512 devices in a mesh: sample: 32 (over x, y, core), cls: 16 (over z).
Axes of the slice: x: 4, y: 4, z: 16, core: 2. Of those that a mesh axis runs over, the one named last changes fastest.
Arguments:
- features: bfloat16 [16384, 2048], P('sample', 'cls'), may hold values from -1.5 to 1.5
- head: bfloat16 [2048, 8192], P('sample', 'cls'), may hold values from -1.5859375 to 1.5859375
- class_cap: bfloat16 [8192], P('cls'), may hold values from 0.5 to 4
Outputs:
- targets: bfloat16 [16384, 8192], P('sample', 'cls')
- grad_features: bfloat16 [16384, 2048], P('sample', 'cls')
- grad_head: bfloat16 [2048, 8192], P('sample', 'cls')
The draws below stay inside these ranges and needn't reach their ends.
All inputs are finite; a program needn't handle non-finite values.
Results may differ from the reference program's by a relative error of at most 0.02.
Values may be sent and summed in bfloat16 or wider, within the bound.
A program may use at most 64 MiB of HBM per device.

```python
import math
import jax
import jax.numpy as jnp
from jax import lax

D = 2048
K = 8192
ITERS = 3
N = 16384
N_SAMPLE = 32
N_CLS = 16


def shard_levels(stream_key, shape, cuts, least, largest):
    factor_of, own = 1.0, jax.random.fold_in(stream_key, 6)
    for position, shards_of in cuts:
        heights = jnp.exp(jax.random.uniform(jax.random.fold_in(own, position), (shards_of,), jnp.float32, least / len(cuts), largest / len(cuts)))
        factor_of = factor_of * jnp.repeat(heights, shape[position] // shards_of).reshape([-1 if axis == position else 1 for axis in range(len(shape))])
    return factor_of


def normal_values(rng, extent, scale, limit, shards=(), dtype=jnp.bfloat16):
    array = scale * jax.random.normal(rng, extent, jnp.float32)
    if shards:
        array = array * shard_levels(rng, extent, shards, -0.22, 0.18)
    return jnp.clip(array, -limit, limit).astype(dtype)


def setup_inputs(seed: int = 0) -> dict:
    key_of = jax.random.split(jax.random.key(seed), 4)
    features = normal_values(key_of[0], (N, D), 0.25, 1.5, ((0, 32), (1, 16)))
    head = normal_values(key_of[1], (D, K), (12.0 / D ** 0.5), 1.5859375, ((0, 32), (1, 16)))
    class_cap = jnp.clip(jnp.exp(math.log(4.0) - 2.0794415 * jax.random.uniform(key_of[2], (K,), jnp.float32) ** shard_levels(key_of[2], (K,), ((0, 16),), -0.2, 0.2)), 0.5, 4.0).astype(jnp.bfloat16)
    return dict(features=features, head=head, class_cap=class_cap)


softcap = 15.0
sharpen = 2.0


def reference(features, head, class_cap):
    row_count = features.shape[0]
    class_count = head.shape[1]
    width = features.shape[1]
    logits = jnp.dot(features, head, preferred_element_type=jnp.float32)
    capped = softcap * jnp.tanh(logits / softcap)
    student = jnp.exp(capped)
    student = student / jnp.sum(student, axis=1, keepdims=True)
    transport = jnp.exp(capped * sharpen)
    ceiling = class_cap.astype(jnp.float32) * (row_count / class_count)
    for iteration in range(ITERS):
        transport = transport / jnp.sum(transport, axis=1, keepdims=True)
        column_mass = jnp.sum(transport, axis=0)
        transport = transport * jnp.minimum(1.0, ceiling / column_mass)
    targets = (transport / jnp.sum(transport, axis=1, keepdims=True)).astype(jnp.bfloat16)
    tanh_slope = 1.0 - (capped / softcap) ** 2
    grad_logits = ((student - targets.astype(jnp.float32)) * tanh_slope).astype(jnp.bfloat16)

    feature_blocks = features.reshape(N_SAMPLE, row_count // N_SAMPLE, width)
    grad_blocks = grad_logits.reshape(N_SAMPLE, row_count // N_SAMPLE, class_count)

    def add_head(total, pair):
        partial_sum = lax.dot_general(pair[0], pair[1], (((0,), (0,)), ((), ())), preferred_element_type=jnp.float32)
        rounded = lax.optimization_barrier(partial_sum.astype(jnp.bfloat16))
        return total + rounded.astype(jnp.float32), None

    head_total, _ = lax.scan(add_head, jnp.zeros((width, class_count), jnp.float32), (feature_blocks, grad_blocks))

    class_local = class_count // N_CLS
    head_blocks = jnp.transpose(head.reshape(width, N_CLS, class_local), (1, 0, 2))
    logit_blocks = jnp.transpose(grad_logits.reshape(row_count, N_CLS, class_local), (1, 0, 2))

    def add_feature(total, pair):
        partial_sum = lax.dot_general(pair[1], pair[0], (((1,), (1,)), ((), ())), preferred_element_type=jnp.float32)
        rounded = lax.optimization_barrier(partial_sum.astype(jnp.bfloat16))
        return total + rounded.astype(jnp.float32), None

    feature_total, _ = lax.scan(add_feature, jnp.zeros((row_count, width), jnp.float32), (head_blocks, logit_blocks))
    return targets, feature_total.astype(jnp.bfloat16), head_total.astype(jnp.bfloat16)
```

```python
import functools
import jax
import jax.numpy as jnp
from jax import lax
from jax.experimental import pallas as pl
from jax.experimental.pallas import tpu as pltpu
from jax.sharding import PartitionSpec as P

ITERS = 3
softcap = 15.0
sharpen = 2.0
MESH = pl.DeviceIdType.MESH
SIDE = 4
BF = jnp.bfloat16
F32 = jnp.float32

OTHERS = sorted(
    ((dx, dy, dc) for dx in range(SIDE) for dy in range(SIDE) for dc in range(2) if dx or dy or dc),
    key=lambda o: -(min(o[0], SIDE - o[0]) + min(o[1], SIDE - o[1]) + 0.5 * o[2]),
)


def kernel(
    rows, width, classes, groups, ratio,
    feat, head, cap,
    tgt, gfeat, ghead,
    fs, hs, ft, ht, acc, stu, plan, slope, grad, rrep,
    part, from_l, from_r,
    qo, core_in, qa, y_in, qb, x_in,
    zs0, zs, zr0, zr, cs, cr,
    ag_send, ag_recv, hx_send, hx_recv, hy_send, hy_recv, hc_send, hc_recv,
    zsend, zrecv, csend, crecv,
    rs_send, rs_recv, qc_send, qc_recv, qy_send, qy_recv, qx_send, qx_recv,
):
    s = lax.axis_index("sample")
    z = lax.axis_index("cls")
    core = lax.rem(s, 2)
    chip = s // 2
    y = lax.rem(chip, SIDE)
    x = chip // SIDE
    way = 1 - 2 * core
    half = rows // 2
    slab = width // groups
    far = groups // 2

    def at(dx, dy, flip=0):
        c = lax.rem(core + flip, 2)
        return ((lax.rem(x + dx + SIDE, SIDE) * SIDE + lax.rem(y + dy + SIDE, SIDE)) * 2 + c, z)

    def along(d):
        return (s, lax.rem(z + d + groups, groups))

    def slot(dx, dy):
        return (lax.rem(x + dx + SIDE, SIDE) * SIDE + lax.rem(y + dy + SIDE, SIDE)) * 2 + core

    def copy(src, dst, ssem, rsem, to):
        return pltpu.make_async_remote_copy(
            src_ref=src, dst_ref=dst, send_sem=ssem, recv_sem=rsem, device_id=to, device_id_type=MESH
        )

    sent = []

    def send(src, dst, ssem, rsem, to):
        c = copy(src, dst, ssem, rsem, to)
        c.start()
        sent.append(c)

    def arrived(ref, rsem):
        copy(ref, ref, rsem, rsem, along(1)).wait_recv()

    barrier = pltpu.get_barrier_semaphore()
    near = [along(1), along(-1), at(1, 0), at(-1, 0), at(0, 1), at(0, -1), at(0, 0, 1)]
    for to in near:
        pl.semaphore_signal(barrier, inc=1, device_id=to, device_id_type=MESH)
    pl.semaphore_wait(barrier, len(near))

    def part_of(ref, h):
        return ref.at[pl.ds(h * half, half)]

    def ring_send(t, h, forward):
        hop = 1 if forward else -1
        k = lax.rem(z - hop * t + groups, groups)
        src = part_of(feat, h) if t == 0 else part_of(fs.at[k], h)
        i = 0 if forward else 1
        send(src, part_of(fs.at[k], h), ag_send.at[i, t, h], ag_recv.at[i, t, h], along(hop))

    def ring_wait(t, h, forward):
        hop = 1 if forward else -1
        k = lax.rem(z - hop * (t + 1) + groups, groups)
        arrived(part_of(fs.at[k], h), ag_recv.at[0 if forward else 1, t, h])

    def ring_step(t):
        for h in range(2):
            for forward in (True, False):
                ring_wait(t - 1, h, forward)
                if t < far - 1 or (h == 0) == forward:
                    ring_send(t, h, forward)

    x_off = (0, -1, 1, 2)
    own = 2 * chip + core

    def to_y(j, src):
        k = slot(x_off[j], 0)
        send(src, hs.at[k], hy_send.at[j, 0], hy_recv.at[j, 0], at(0, 1))
        send(src, hs.at[k], hy_send.at[j, 1], hy_recv.at[j, 1], at(0, -1))

    def to_core(j, i, src):
        k = slot(x_off[j], x_off[i])
        send(src, hs.at[k], hc_send.at[j, i], hc_recv.at[j, i], at(0, 0, 1))

    for h in range(2):
        ring_send(0, h, True)
        ring_send(0, h, False)
    send(head, hs.at[own], hx_send.at[0], hx_recv.at[0], at(1, 0))
    send(head, hs.at[own], hx_send.at[1], hx_recv.at[1], at(-1, 0))
    to_y(0, head)
    to_core(0, 0, head)
    fs[z] = feat[...]
    hs[own] = head[...]

    behind = slot(-way, 0)
    arrived(hs.at[behind], hx_recv.at[core])
    send(hs.at[behind], hs.at[behind], hx_send.at[2], hx_recv.at[2], at(way, 0))
    ahead = slot(way, 0)
    arrived(hs.at[ahead], hx_recv.at[1 - core])
    for j in (1, 2):
        to_y(j, hs.at[slot(x_off[j], 0)])
        to_core(j, 0, hs.at[slot(x_off[j], 0)])
    ring_step(1)
    arrived(hs.at[slot(2, 0)], hx_recv.at[2])
    to_y(3, hs.at[slot(2, 0)])
    to_core(3, 0, hs.at[slot(2, 0)])

    def y_pair(j):
        k = slot(x_off[j], -way)
        arrived(hs.at[k], hy_recv.at[j, core])
        send(hs.at[k], hs.at[k], hy_send.at[j, 2], hy_recv.at[j, 2], at(0, way))
        arrived(hs.at[slot(x_off[j], way)], hy_recv.at[j, 1 - core])
        to_core(j, 1, hs.at[slot(x_off[j], -1)])
        to_core(j, 2, hs.at[slot(x_off[j], 1)])

    def y_far(j):
        k = slot(x_off[j], 2)
        arrived(hs.at[k], hy_recv.at[j, 2])
        to_core(j, 3, hs.at[k])

    y_pair(0)
    ring_step(2)
    y_far(0)
    y_pair(1)
    ring_step(3)
    y_far(1)
    y_pair(2)
    ring_step(4)
    y_far(2)
    y_pair(3)
    ring_step(5)
    y_far(3)

    def head_of(k):
        return hs[pl.ds(2 * k, 2)].reshape(slab, classes)

    def logits_of(a, b, r0, n):
        left = jnp.concatenate([fs[a, pl.ds(r0, n), :], fs[b, pl.ds(r0, n), :]], axis=1)
        right = jnp.concatenate([head_of(a), head_of(b)], axis=0)
        return jnp.dot(left, right, preferred_element_type=F32)

    def around(d):
        return lax.rem(z - d + groups, groups), lax.rem(z + d, groups)

    ring_step(6)
    for j in range(4):
        for i in range(4):
            k = (lax.rem(x + x_off[j] + SIDE, SIDE) * SIDE + lax.rem(y + x_off[i] + SIDE, SIDE)) * 2 + (1 - core)
            arrived(hs.at[k], hc_recv.at[j, i])
    acc[...] = logits_of(*around(1), 0, rows)
    for d in (2, 3, 4):
        acc[...] += logits_of(*around(d), 0, rows)
    ring_step(7)
    for d in (5, 6, 7):
        acc[...] += logits_of(*around(d), 0, rows)
    ring_wait(far - 1, 0, True)
    ring_wait(far - 1, 1, False)

    lanes = 128
    tiles = classes // lanes

    def lane_tiles(v):
        return [v[:, i * lanes:(i + 1) * lanes] for i in range(tiles)]

    def turned_sum(v):
        return jnp.sum(sum(lane_tiles(v)[1:], lane_tiles(v)[0]).T, axis=0, keepdims=True)

    opposite = lax.rem(z + far, groups)
    for r0 in range(0, rows, lanes):
        block = pl.ds(r0, lanes)
        tanh = jnp.tanh((acc[block, :] + logits_of(z, opposite, r0, lanes)) / softcap)
        student = jnp.exp(softcap * tanh)
        transport = student * student
        stu[block, :] = student
        plan[block, :] = transport
        slope[block, :] = 1.0 - tanh * tanh
        zs0[:, r0:r0 + lanes] = turned_sum(transport)
        zs0[:, rows + r0:rows + r0 + lanes] = turned_sum(student)

    z_order = sorted(range(1, groups), key=lambda d: -min(d, groups - d))

    def z_exchange(mine, theirs, i):
        for d in z_order:
            copy(mine, theirs.at[d - 1], zsend.at[i], zrecv.at[i], along(d)).start()

    def z_total(mine, theirs, i):
        copy(theirs, theirs, zsend.at[i], zrecv.at[i], along(1)).wait_recv()
        return mine[...] + jnp.sum(theirs[...], axis=0)

    def c_exchange(mine, theirs, i):
        for n, (dx, dy, dc) in enumerate(OTHERS):
            copy(mine, theirs.at[n], csend.at[i], crecv.at[i], at(dx, dy, dc)).start()

    def c_total(mine, theirs, i):
        copy(theirs, theirs, csend.at[i], crecv.at[i], along(1)).wait_recv()
        return mine[...] + jnp.sum(theirs[...], axis=0)

    def upright(row, r0):
        return jnp.broadcast_to(row[:, r0:r0 + lanes], (lanes, lanes)).T

    z_exchange(zs0, zr0, 0)

    def turn(k, carry):
        t = fs[k].T
        ft[0, lax.rem(k, SIDE), k // SIDE] = t[: slab // 2]
        ft[1, lax.rem(k, SIDE), k // SIDE] = t[slab // 2:]
        ht[k] = head_of(k).T
        return carry

    lax.fori_loop(0, groups, turn, 0)

    ceiling = cap[...].astype(F32) * ratio
    scale = jnp.ones((1, classes), F32)
    both = z_total(zs0, zr0, 0)
    mass = both[:, :rows]
    student_mass = both[:, rows:]
    for it in range(ITERS):
        inverse = 1.0 / mass
        column = jnp.zeros((1, classes), F32)
        for r0 in range(0, rows, lanes):
            up = upright(inverse, r0)
            rep = jnp.concatenate([up] * tiles, axis=1)
            column += jnp.sum(plan[pl.ds(r0, lanes), :] * rep, axis=0, keepdims=True)
        cs[it] = column
        c_exchange(cs.at[it], cr.at[it], it)
        total = c_total(cs.at[it], cr.at[it], it)
        scale = jnp.minimum(scale, ceiling / total)
        for r0 in range(0, rows, lanes):
            zs[it, :, r0:r0 + lanes] = turned_sum(plan[pl.ds(r0, lanes), :] * scale)
        z_exchange(zs.at[it], zr.at[it], it + 1)
        mass = z_total(zs.at[it], zr.at[it], it + 1)

    inverse = 1.0 / mass
    student_inverse = 1.0 / student_mass
    for r0 in range(0, rows, lanes):
        block = pl.ds(r0, lanes)
        up = jnp.concatenate([upright(inverse, r0)] * tiles, axis=1)
        sup = jnp.concatenate([upright(student_inverse, r0)] * tiles, axis=1)
        targets = (plan[block, :] * up * scale).astype(BF)
        tgt[block, :] = targets
        grad[block, :] = ((stu[block, :] * sup - targets.astype(F32)) * slope[block, :]).astype(BF)

    def share_pair(d):
        right = lax.rem(z + d, groups)
        left = lax.rem(z - d + groups, groups) if d < far else z
        both = jnp.concatenate([ht[right], ht[left]], axis=1)
        out = jnp.dot(grad[...], both, preferred_element_type=F32).astype(BF)
        part[d] = out[:, :slab]
        part[groups - d if d < far else 0] = out[:, slab:]

    def rs_send_to(d, h, right):
        i = 0 if right else 1
        src = part.at[d if right or d == far else groups - d]
        dst = from_l if right else from_r
        send(part_of(src, h), part_of(dst.at[d - 1], h), rs_send.at[i, d - 1, h], rs_recv.at[i, d - 1, h],
             along(1 if right else -1))

    def rs_add(d, h, right):
        i = 0 if right else 1
        got = (from_l if right else from_r).at[d]
        mine = part.at[d if right else groups - d]
        arrived(part_of(got, h), rs_recv.at[i, d, h])
        at_h = pl.ds(h * half, half)
        mine[at_h, :] = (mine[at_h, :].astype(F32) + got[at_h, :].astype(F32)).astype(BF)
        rs_send_to(d, h, right)

    def rs_step(d):
        for h in range(2):
            for right in (True, False):
                if d < far - 1 or (h == 0) == right:
                    rs_add(d, h, right)

    def head_share(c, i):
        lhs = ft[c, lax.rem(y + i, SIDE)].reshape(SIDE * slab // 2, rows)
        out = jnp.dot(lhs, grad[...], preferred_element_type=F32).astype(BF)
        return out.reshape(SIDE, slab // 2, classes)

    share_pair(far)
    rs_send_to(far, 0, True)
    rs_send_to(far, 1, False)
    share_pair(far - 1)
    rs_send_to(far - 1, 1, True)
    rs_send_to(far - 1, 0, False)
    for i in (2, 1, 3, 0):
        qo[i] = head_share(1 - core, i)
        send(qo.at[i], core_in.at[i], qc_send.at[i], qc_recv.at[i], at(0, 0, 1))
    share_pair(6)
    rs_step(7)
    for i in (2, 1, 3, 0):
        qa[i] = head_share(core, i)
    share_pair(5)
    rs_step(6)

    def summed(*refs):
        out = refs[0].astype(F32)
        for r in refs[1:]:
            out = out + r.astype(F32)
        return out.astype(BF)

    fwd = 1 + 2 * core
    bwd = 3 - 2 * core
    for i in (2, 1, 3, 0):
        arrived(core_in.at[i], qc_recv.at[i])
        qa[i] = summed(qa[i], core_in[i])
        if i == 2:
            send(qa.at[2], y_in.at[0], qy_send.at[0], qy_recv.at[0], at(0, way))
        if i == 3:
            send(qa.at[bwd], y_in.at[1], qy_send.at[1], qy_recv.at[1], at(0, -way))
    share_pair(4)
    share_pair(3)
    rs_step(5)
    share_pair(2)
    share_pair(1)
    arrived(y_in.at[0], qy_recv.at[0])
    qa[fwd] = summed(qa[fwd], y_in[0])
    send(qa.at[fwd], y_in.at[2], qy_send.at[2], qy_recv.at[2], at(0, way))
    rs_step(4)
    rs_step(3)
    arrived(y_in.at[1], qy_recv.at[1])
    arrived(y_in.at[2], qy_recv.at[2])
    qb[...] = summed(qa[0], y_in[1], y_in[2])

    def x_of(d):
        return lax.rem(x + d + SIDE, SIDE)

    send(qb.at[x_of(2)], x_in.at[0], qx_send.at[0], qx_recv.at[0], at(way, 0))
    send(qb.at[x_of(-way)], x_in.at[1], qx_send.at[1], qx_recv.at[1], at(-way, 0))
    rs_step(2)
    arrived(x_in.at[0], qx_recv.at[0])
    qb[x_of(way)] = summed(qb[x_of(way)], x_in[0])
    send(qb.at[x_of(way)], x_in.at[2], qx_send.at[2], qx_recv.at[2], at(way, 0))
    rs_step(1)
    arrived(x_in.at[1], qx_recv.at[1])
    arrived(x_in.at[2], qx_recv.at[2])
    ghead[...] = summed(qb[x], x_in[1], x_in[2])
    for h in range(2):
        arrived(part_of(from_l.at[0], h), rs_recv.at[0, 0, h])
        arrived(part_of(from_r.at[0], h), rs_recv.at[1, 0, h])
    gfeat[...] = summed(part[0], from_l[0], from_r[0])

    copy(zr0, zr0, zsend.at[0], zrecv.at[0], along(1)).wait_send()
    for it in range(ITERS):
        copy(zr.at[it], zr.at[it], zsend.at[it + 1], zrecv.at[it + 1], along(1)).wait_send()
        copy(cr.at[it], cr.at[it], csend.at[it], crecv.at[it], along(1)).wait_send()
    for c in sent:
        c.wait_send()


def solution(mesh):
    groups = mesh.shape["cls"]
    samples = mesh.shape["sample"]

    def per_device(features, head, class_cap):
        rows, slab = features.shape
        depth, classes = head.shape
        width = slab * groups
        chips = samples // 2
        far = groups // 2
        ratio = rows * samples / (classes * groups)
        V = pltpu.VMEM
        dma = pltpu.SemaphoreType.DMA
        scratch = [
            V((groups, rows, slab), BF), V((samples, depth, classes), BF),
            V((2, SIDE, SIDE, depth, rows), BF), V((groups, classes, slab), BF),
            V((rows, classes), F32), V((rows, classes), F32), V((rows, classes), F32), V((rows, classes), F32),
            V((rows, classes), BF), V((8, 128), F32),
            V((groups, rows, slab), BF), V((far, rows, slab), BF), V((far, rows, slab), BF),
            V((SIDE, SIDE, depth, classes), BF), V((SIDE, SIDE, depth, classes), BF),
            V((SIDE, SIDE, depth, classes), BF), V((3, SIDE, depth, classes), BF),
            V((SIDE, depth, classes), BF), V((3, depth, classes), BF),
            V((1, 2 * rows), F32), V((ITERS, 1, rows), F32),
            V((groups - 1, 1, 2 * rows), F32), V((ITERS, groups - 1, 1, rows), F32),
            V((ITERS, 1, classes), F32), V((ITERS, samples - 1, 1, classes), F32),
            dma((2, far, 2)), dma((2, far, 2)), dma((3,)), dma((3,)), dma((4, 3)), dma((4, 3)), dma((4, 4)), dma((4, 4)),
            dma((ITERS + 1,)), dma((ITERS + 1,)), dma((ITERS,)), dma((ITERS,)),
            dma((2, far, 2)), dma((2, far, 2)), dma((4,)), dma((4,)), dma((3,)), dma((3,)), dma((3,)), dma((3,)),
        ]
        vmem = pl.BlockSpec(memory_space=pltpu.VMEM)
        return pl.pallas_call(
            functools.partial(kernel, rows, width, classes, groups, ratio),
            out_shape=(
                jax.ShapeDtypeStruct((rows, classes), BF),
                jax.ShapeDtypeStruct((rows, slab), BF),
                jax.ShapeDtypeStruct((depth, classes), BF),
            ),
            in_specs=[vmem] * 3,
            out_specs=(vmem,) * 3,
            scratch_shapes=scratch,
            compiler_params=pltpu.CompilerParams(
                collective_id=0, has_side_effects=True, vmem_limit_bytes=48 << 20
            ),
        )(features, head, class_cap.reshape(1, classes))

    return jax.shard_map(
        per_device,
        mesh=mesh,
        in_specs=(P("sample", "cls"), P("sample", "cls"), P("cls")),
        out_specs=(P("sample", "cls"), P("sample", "cls"), P("sample", "cls")),
        check_vma=False,
    )
```

```python
import functools
import jax
import jax.numpy as jnp
from jax import lax
from jax.experimental import pallas as pl
from jax.experimental.pallas import tpu as pltpu
from jax.sharding import PartitionSpec as P

ITERS = 3
softcap = 15.0
sharpen = 2.0
MESH = pl.DeviceIdType.MESH
SIDE = 4
PIECES = 4
BF = jnp.bfloat16
F32 = jnp.float32

OTHERS = sorted(
    ((dx, dy, dc) for dx in range(SIDE) for dy in range(SIDE) for dc in range(2) if dx or dy or dc),
    key=lambda o: -(min(o[0], SIDE - o[0]) + min(o[1], SIDE - o[1]) + 0.5 * o[2]),
)


def kernel(
    rows, width, classes, groups, ratio,
    feat, head, cap_in,
    tgt, gfeat, ghead,
    fs, hs, ft, ht, acc, stu, plan, slope, grad,
    part, from_l, from_r,
    qo, core_in, qa, y_in, qb, x_in,
    zs0, zs, zr0, zr, cs, cr,
    ag_send, ag_recv, hx_send, hx_recv, hy_send, hy_recv, hc_send, hc_recv,
    zsend, zrecv, csend, crecv, cap, local,
    rs_send, rs_recv, qc_send, qc_recv, qy_send, qy_recv, qx_send, qx_recv,
):
    s = lax.axis_index("sample")
    z = lax.axis_index("cls")
    core = lax.rem(s, 2)
    chip = s // 2
    y = lax.rem(chip, SIDE)
    x = chip // SIDE
    way = 1 - 2 * core
    n = rows // PIECES
    slab = width // groups
    far = groups // 2

    def at(dx, dy, flip=0):
        c = lax.rem(core + flip, 2)
        return ((lax.rem(x + dx + SIDE, SIDE) * SIDE + lax.rem(y + dy + SIDE, SIDE)) * 2 + c, z)

    def along(d):
        return (s, lax.rem(z + d + groups, groups))

    def slot(dx, dy):
        return (lax.rem(x + dx + SIDE, SIDE) * SIDE + lax.rem(y + dy + SIDE, SIDE)) * 2 + core

    def copy(src, dst, ssem, rsem, to):
        return pltpu.make_async_remote_copy(
            src_ref=src, dst_ref=dst, send_sem=ssem, recv_sem=rsem, device_id=to, device_id_type=MESH
        )

    sent = []

    def send(src, dst, ssem, rsem, to):
        c = copy(src, dst, ssem, rsem, to)
        c.start()
        sent.append(c)

    def arrived(ref, rsem):
        copy(ref, ref, rsem, rsem, along(1)).wait_recv()

    barrier = pltpu.get_barrier_semaphore()
    near = [along(1), along(-1), at(1, 0), at(-1, 0), at(0, 1), at(0, -1), at(0, 0, 1)]
    for to in near:
        pl.semaphore_signal(barrier, inc=1, device_id=to, device_id_type=MESH)
    pl.semaphore_wait(barrier, len(near))

    def part_of(ref, q):
        return ref.at[pl.ds(q * n, n)]

    right_order = tuple(range(PIECES))
    left_order = right_order[PIECES // 2:] + right_order[:PIECES // 2]

    def halfway(q, forward):
        return (q < PIECES // 2) == forward

    def ring_send(t, q, forward):
        hop = 1 if forward else -1
        k = lax.rem(z - hop * t + groups, groups)
        src = part_of(feat, q) if t == 0 else part_of(fs.at[k], q)
        i = 0 if forward else 1
        send(src, part_of(fs.at[k], q), ag_send.at[i, t, q], ag_recv.at[i, t, q], along(hop))

    def ring_wait(t, q, forward):
        hop = 1 if forward else -1
        k = lax.rem(z - hop * (t + 1) + groups, groups)
        arrived(part_of(fs.at[k], q), ag_recv.at[0 if forward else 1, t, q])

    def ring_step(t, pieces=range(PIECES)):
        for p in pieces:
            for forward, q in ((True, right_order[p]), (False, left_order[p])):
                ring_wait(t - 1, q, forward)
                if t < far - 1 or halfway(q, forward):
                    ring_send(t, q, forward)

    x_off = (0, -1, 1, 2)
    own = 2 * chip + core

    def to_y(j, src):
        k = slot(x_off[j], 0)
        send(src, hs.at[k], hy_send.at[j, 0], hy_recv.at[j, 0], at(0, 1))
        send(src, hs.at[k], hy_send.at[j, 1], hy_recv.at[j, 1], at(0, -1))

    def to_core(j, i, src):
        k = slot(x_off[j], x_off[i])
        send(src, hs.at[k], hc_send.at[j, i], hc_recv.at[j, i], at(0, 0, 1))

    for p in range(PIECES):
        ring_send(0, right_order[p], True)
        ring_send(0, left_order[p], False)
    send(head, hs.at[own], hx_send.at[0], hx_recv.at[0], at(1, 0))
    send(head, hs.at[own], hx_send.at[1], hx_recv.at[1], at(-1, 0))
    to_y(0, head)
    to_core(0, 0, head)
    mine = [
        pltpu.make_async_copy(feat, fs.at[z], local.at[0]),
        pltpu.make_async_copy(head, hs.at[own], local.at[1]),
        pltpu.make_async_copy(cap_in, cap, local.at[2]),
    ]
    for c in mine:
        c.start()

    def x_near():
        behind = slot(-way, 0)
        arrived(hs.at[behind], hx_recv.at[core])
        send(hs.at[behind], hs.at[behind], hx_send.at[2], hx_recv.at[2], at(way, 0))
        arrived(hs.at[slot(way, 0)], hx_recv.at[1 - core])
        for j in (1, 2):
            to_y(j, hs.at[slot(x_off[j], 0)])
            to_core(j, 0, hs.at[slot(x_off[j], 0)])

    def x_far():
        arrived(hs.at[slot(2, 0)], hx_recv.at[2])
        to_y(3, hs.at[slot(2, 0)])
        to_core(3, 0, hs.at[slot(2, 0)])

    def y_pair(j):
        k = slot(x_off[j], -way)
        arrived(hs.at[k], hy_recv.at[j, core])
        send(hs.at[k], hs.at[k], hy_send.at[j, 2], hy_recv.at[j, 2], at(0, way))
        arrived(hs.at[slot(x_off[j], way)], hy_recv.at[j, 1 - core])
        to_core(j, 1, hs.at[slot(x_off[j], -1)])
        to_core(j, 2, hs.at[slot(x_off[j], 1)])

    def y_far(j):
        k = slot(x_off[j], 2)
        arrived(hs.at[k], hy_recv.at[j, 2])
        to_core(j, 3, hs.at[k])

    x_near()
    ring_step(1)
    y_pair(0)
    ring_step(2, range(PIECES // 2))
    x_far()
    ring_step(2, range(PIECES // 2, PIECES))
    y_far(0)
    y_pair(1)
    ring_step(3, range(PIECES // 2))
    y_pair(2)
    ring_step(3, range(PIECES // 2, PIECES))
    y_far(1)
    y_pair(3)
    ring_step(4, range(PIECES // 2))
    y_far(2)
    ring_step(4, range(PIECES // 2, PIECES))
    y_far(3)
    ring_step(5)

    def head_of(k):
        return hs[pl.ds(2 * k, 2)].reshape(slab, classes)

    def logits_of(slots, r0, count):
        left = jnp.concatenate([fs[k, pl.ds(r0, count), :] for k in slots], axis=1)
        right = jnp.concatenate([head_of(k) for k in slots], axis=0)
        return jnp.dot(left, right, preferred_element_type=F32)

    def around(*distances):
        return [lax.rem(z + d, groups) for e in distances for d in (groups - e, e)]

    for j in range(4):
        for i in range(4):
            k = (lax.rem(x + x_off[j] + SIDE, SIDE) * SIDE + lax.rem(y + x_off[i] + SIDE, SIDE)) * 2 + (1 - core)
            arrived(hs.at[k], hc_recv.at[j, i])
    for c in mine:
        c.wait()
    acc[...] = logits_of(around(1, 2), 0, rows)
    ring_step(6, range(PIECES // 2))
    acc[...] += logits_of(around(3, 4), 0, rows)
    ring_step(6, range(PIECES // 2, PIECES))
    acc[...] += logits_of(around(5), 0, rows)
    ring_step(7, range(PIECES // 2))
    acc[...] += logits_of(around(6), 0, rows)
    ring_step(7, range(PIECES // 2, PIECES))
    acc[...] += logits_of(around(7), 0, rows)

    lanes = 128
    tiles = classes // lanes

    def lane_tiles(v):
        return [v[:, i * lanes:(i + 1) * lanes] for i in range(tiles)]

    def turned_sum(v):
        return jnp.sum(sum(lane_tiles(v)[1:], lane_tiles(v)[0]).T, axis=0, keepdims=True)

    opposite = lax.rem(z + far, groups)
    start_order = [q for pair in zip(right_order[: PIECES // 2], left_order[: PIECES // 2]) for q in pair]
    for q in start_order:
        ring_wait(far - 1, q, halfway(q, True))
        r0 = q * n
        block = pl.ds(r0, n)
        tanh = jnp.tanh((acc[block, :] + logits_of([z, opposite], r0, n)) / softcap)
        student = jnp.exp(softcap * tanh)
        transport = student * student
        stu[block, :] = student
        plan[block, :] = transport
        slope[block, :] = 1.0 - tanh * tanh
        zs0[:, r0:r0 + n] = turned_sum(transport)
        zs0[:, rows + r0:rows + r0 + n] = turned_sum(student)

    z_order = sorted(range(1, groups), key=lambda d: -min(d, groups - d))

    def z_exchange(mine, theirs, i):
        for d in z_order:
            copy(mine, theirs.at[d - 1], zsend.at[i], zrecv.at[i], along(d)).start()

    def z_total(mine, theirs, i):
        copy(theirs, theirs, zsend.at[i], zrecv.at[i], along(1)).wait_recv()
        return mine[...] + jnp.sum(theirs[...], axis=0)

    def c_exchange(mine, theirs, i):
        for n, (dx, dy, dc) in enumerate(OTHERS):
            copy(mine, theirs.at[n], csend.at[i], crecv.at[i], at(dx, dy, dc)).start()

    def c_total(mine, theirs, i):
        copy(theirs, theirs, csend.at[i], crecv.at[i], along(1)).wait_recv()
        return mine[...] + jnp.sum(theirs[...], axis=0)

    def upright(row, r0):
        return jnp.broadcast_to(row[:, r0:r0 + lanes], (lanes, lanes)).T

    z_exchange(zs0, zr0, 0)

    def turn(k, carry):
        t = fs[k].T
        ft[0, lax.rem(k, SIDE), k // SIDE] = t[: slab // 2]
        ft[1, lax.rem(k, SIDE), k // SIDE] = t[slab // 2:]
        ht[k] = head_of(k).T
        return carry

    lax.fori_loop(0, groups, turn, 0)

    ceiling = cap[...].astype(F32).reshape(1, classes) * ratio
    scale = jnp.ones((1, classes), F32)
    both = z_total(zs0, zr0, 0)
    mass = both[:, :rows]
    student_mass = both[:, rows:]
    for it in range(ITERS):
        inverse = 1.0 / mass
        column = jnp.zeros((1, classes), F32)
        for r0 in range(0, rows, lanes):
            up = upright(inverse, r0)
            rep = jnp.concatenate([up] * tiles, axis=1)
            column += jnp.sum(plan[pl.ds(r0, lanes), :] * rep, axis=0, keepdims=True)
        cs[it] = column
        c_exchange(cs.at[it], cr.at[it], it)
        total = c_total(cs.at[it], cr.at[it], it)
        scale = jnp.minimum(scale, ceiling / total)
        for r0 in range(0, rows, lanes):
            zs[it, :, r0:r0 + lanes] = turned_sum(plan[pl.ds(r0, lanes), :] * scale)
        z_exchange(zs.at[it], zr.at[it], it + 1)
        mass = z_total(zs.at[it], zr.at[it], it + 1)

    def rs_send_to(d, q, right):
        i = 0 if right else 1
        src = part.at[d if right or d == far else groups - d]
        dst = from_l if right else from_r
        send(part_of(src, q), part_of(dst.at[d - 1], q), rs_send.at[i, d - 1, q], rs_recv.at[i, d - 1, q],
             along(1 if right else -1))

    def rs_add(d, q, right):
        i = 0 if right else 1
        got = (from_l if right else from_r).at[d]
        mine = part.at[d if right else groups - d]
        arrived(part_of(got, q), rs_recv.at[i, d, q])
        block = pl.ds(q * n, n)
        mine[block, :] = (mine[block, :].astype(F32) + got[block, :].astype(F32)).astype(BF)
        rs_send_to(d, q, right)

    def rs_step(d):
        if d == far - 1:
            pairs = [(right_order[p], left_order[p]) for p in range(PIECES // 2)]
        else:
            pairs = [(left_order[p], right_order[p]) for p in range(PIECES)]
        for to_right, to_left in pairs:
            rs_add(d, to_right, True)
            rs_add(d, to_left, False)

    def share_pair(d, r0=0, count=rows):
        right = lax.rem(z + d, groups)
        left = lax.rem(z - d + groups, groups) if d < far else z
        both = jnp.concatenate([ht[right], ht[left]], axis=1)
        block = pl.ds(r0, count)
        out = jnp.dot(grad[block, :], both, preferred_element_type=F32).astype(BF)
        part[d, block, :] = out[:, :slab]
        part[groups - d if d < far else 0, block, :] = out[:, slab:]

    inverse = 1.0 / mass
    student_inverse = 1.0 / student_mass
    for q in start_order:
        r0 = q * n
        block = pl.ds(r0, n)
        up = jnp.concatenate([upright(inverse, r0)] * tiles, axis=1)
        sup = jnp.concatenate([upright(student_inverse, r0)] * tiles, axis=1)
        targets = (plan[block, :] * up * scale).astype(BF)
        tgt[block, :] = targets
        grad[block, :] = ((stu[block, :] * sup - targets.astype(F32)) * slope[block, :]).astype(BF)
        share_pair(far, r0, n)
        rs_send_to(far, q, halfway(q, True))

    def head_share(c, i):
        lhs = ft[c, lax.rem(y + i, SIDE)].reshape(SIDE * slab // 2, rows)
        out = jnp.dot(lhs, grad[...], preferred_element_type=F32).astype(BF)
        return out.reshape(SIDE, slab // 2, classes)

    share_pair(far - 1)
    for p in range(PIECES // 2):
        rs_send_to(far - 1, left_order[p], True)
        rs_send_to(far - 1, right_order[p], False)
    for i in (2, 1, 3, 0):
        qo[i] = head_share(1 - core, i)
        send(qo.at[i], core_in.at[i], qc_send.at[i], qc_recv.at[i], at(0, 0, 1))
    share_pair(6)
    rs_step(7)
    for i in (2, 1, 3, 0):
        qa[i] = head_share(core, i)
    share_pair(5)
    rs_step(6)

    def summed(*refs):
        out = refs[0].astype(F32)
        for r in refs[1:]:
            out = out + r.astype(F32)
        return out.astype(BF)

    fwd = 1 + 2 * core
    bwd = 3 - 2 * core
    for i in (2, 1, 3, 0):
        arrived(core_in.at[i], qc_recv.at[i])
        qa[i] = summed(qa[i], core_in[i])
        if i == 2:
            send(qa.at[2], y_in.at[0], qy_send.at[0], qy_recv.at[0], at(0, way))
        if i == 3:
            send(qa.at[bwd], y_in.at[1], qy_send.at[1], qy_recv.at[1], at(0, -way))
    share_pair(4)
    share_pair(3)
    rs_step(5)
    share_pair(2)
    share_pair(1)
    arrived(y_in.at[0], qy_recv.at[0])
    qa[fwd] = summed(qa[fwd], y_in[0])
    send(qa.at[fwd], y_in.at[2], qy_send.at[2], qy_recv.at[2], at(0, way))
    rs_step(4)
    rs_step(3)
    arrived(y_in.at[1], qy_recv.at[1])
    arrived(y_in.at[2], qy_recv.at[2])
    qb[...] = summed(qa[0], y_in[1], y_in[2])

    def x_of(d):
        return lax.rem(x + d + SIDE, SIDE)

    send(qb.at[x_of(2)], x_in.at[0], qx_send.at[0], qx_recv.at[0], at(way, 0))
    send(qb.at[x_of(-way)], x_in.at[1], qx_send.at[1], qx_recv.at[1], at(-way, 0))
    rs_step(2)
    arrived(x_in.at[0], qx_recv.at[0])
    qb[x_of(way)] = summed(qb[x_of(way)], x_in[0])
    send(qb.at[x_of(way)], x_in.at[2], qx_send.at[2], qx_recv.at[2], at(way, 0))
    rs_step(1)
    arrived(x_in.at[1], qx_recv.at[1])
    arrived(x_in.at[2], qx_recv.at[2])
    ghead[...] = summed(qb[x], x_in[1], x_in[2])
    for p in range(PIECES):
        arrived(part_of(from_l.at[0], left_order[p]), rs_recv.at[0, 0, left_order[p]])
        arrived(part_of(from_r.at[0], right_order[p]), rs_recv.at[1, 0, right_order[p]])
    gfeat[...] = summed(part[0], from_l[0], from_r[0])

    copy(zr0, zr0, zsend.at[0], zrecv.at[0], along(1)).wait_send()
    for it in range(ITERS):
        copy(zr.at[it], zr.at[it], zsend.at[it + 1], zrecv.at[it + 1], along(1)).wait_send()
        copy(cr.at[it], cr.at[it], csend.at[it], crecv.at[it], along(1)).wait_send()
    for c in sent:
        c.wait_send()


def store_kernel(*refs):
    count = len(refs) // 2
    copies = [pltpu.make_async_copy(refs[i], refs[count + i], refs[-1].at[i]) for i in range(count)]
    for c in copies:
        c.start()
    for c in copies:
        c.wait()


def store(results):
    return pl.pallas_call(
        store_kernel,
        out_shape=tuple(jax.ShapeDtypeStruct(r.shape, r.dtype) for r in results),
        in_specs=[pl.BlockSpec(memory_space=pltpu.VMEM)] * len(results),
        out_specs=(pl.BlockSpec(memory_space=pltpu.HBM),) * len(results),
        scratch_shapes=[pltpu.SemaphoreType.DMA((len(results),))],
        compiler_params=pltpu.CompilerParams(vmem_limit_bytes=4 << 20),
    )(*results)


def solution(mesh):
    groups = mesh.shape["cls"]
    samples = mesh.shape["sample"]

    def per_device(features, head, class_cap):
        rows, slab = features.shape
        depth, classes = head.shape
        width = slab * groups
        chips = samples // 2
        far = groups // 2
        ratio = rows * samples / (classes * groups)
        V = pltpu.VMEM
        dma = pltpu.SemaphoreType.DMA
        scratch = [
            V((groups, rows, slab), BF), V((samples, depth, classes), BF),
            V((2, SIDE, SIDE, depth, rows), BF), V((groups, classes, slab), BF),
            V((rows, classes), F32), V((rows, classes), F32), V((rows, classes), F32), V((rows, classes), F32),
            V((rows, classes), BF),
            V((groups, rows, slab), BF), V((far, rows, slab), BF), V((far, rows, slab), BF),
            V((SIDE, SIDE, depth, classes), BF), V((SIDE, SIDE, depth, classes), BF),
            V((SIDE, SIDE, depth, classes), BF), V((3, SIDE, depth, classes), BF),
            V((SIDE, depth, classes), BF), V((3, depth, classes), BF),
            V((1, 2 * rows), F32), V((ITERS, 1, rows), F32),
            V((groups - 1, 1, 2 * rows), F32), V((ITERS, groups - 1, 1, rows), F32),
            V((ITERS, 1, classes), F32), V((ITERS, samples - 1, 1, classes), F32),
            dma((2, far, PIECES)), dma((2, far, PIECES)), dma((3,)), dma((3,)), dma((4, 3)), dma((4, 3)), dma((4, 4)), dma((4, 4)),
            dma((ITERS + 1,)), dma((ITERS + 1,)), dma((ITERS,)), dma((ITERS,)),
            V((classes,), BF), dma((3,)),
            dma((2, far, PIECES)), dma((2, far, PIECES)), dma((4,)), dma((4,)), dma((3,)), dma((3,)), dma((3,)), dma((3,)),
        ]
        vmem = pl.BlockSpec(memory_space=pltpu.VMEM)
        hbm = pl.BlockSpec(memory_space=pltpu.HBM)
        results = pl.pallas_call(
            functools.partial(kernel, rows, width, classes, groups, ratio),
            out_shape=(
                jax.ShapeDtypeStruct((rows, classes), BF),
                jax.ShapeDtypeStruct((rows, slab), BF),
                jax.ShapeDtypeStruct((depth, classes), BF),
            ),
            in_specs=[hbm] * 3,
            out_specs=(vmem,) * 3,
            scratch_shapes=scratch,
            compiler_params=pltpu.CompilerParams(
                collective_id=0, has_side_effects=True, vmem_limit_bytes=48 << 20
            ),
        )(features, head, class_cap)
        return store(results)

    return jax.shard_map(
        per_device,
        mesh=mesh,
        in_specs=(P("sample", "cls"), P("sample", "cls"), P("cls")),
        out_specs=(P("sample", "cls"), P("sample", "cls"), P("sample", "cls")),
        check_vma=False,
    )
```

```python
import functools
import jax
import jax.numpy as jnp
from jax import lax
from jax.experimental import pallas as pl
from jax.experimental.pallas import tpu as pltpu
from jax.sharding import PartitionSpec as P

ITERS = 3
softcap = 15.0
sharpen = 2.0
MESH = pl.DeviceIdType.MESH
SIDE = 4
PIECES = 4
BF = jnp.bfloat16
F32 = jnp.float32

OTHERS = sorted(
    ((dx, dy, dc) for dx in range(SIDE) for dy in range(SIDE) for dc in range(2) if dx or dy or dc),
    key=lambda o: -(min(o[0], SIDE - o[0]) + min(o[1], SIDE - o[1]) + 0.5 * o[2]),
)


def kernel(
    rows, width, classes, groups, ratio,
    feat, head, cap_in,
    tgt, gfeat, ghead,
    fs, hs, fta, ftb, ht, acc, stu, plan, slope, grad,
    part, from_l, from_r,
    qo, core_in, qa, first_in, qb, second_in,
    zs0, zs, zr0, zr, cs, cr,
    ag_send, ag_recv, hx_send, hx_recv, hy_send, hy_recv, hc_send, hc_recv,
    zsend, zrecv, csend, crecv, cap, local,
    rs_send, rs_recv, qc_send, qc_recv, q1_send, q1_recv, q2_send, q2_recv,
):
    s = lax.axis_index("sample")
    z = lax.axis_index("cls")
    core = lax.rem(s, 2)
    chip = s // 2
    y = lax.rem(chip, SIDE)
    x = chip // SIDE
    way = 1 - 2 * core
    n = rows // PIECES
    slab = width // groups
    far = groups // 2
    quarter = slab // 4

    def at(dx, dy, flip=0):
        c = lax.rem(core + flip, 2)
        return ((lax.rem(x + dx + SIDE, SIDE) * SIDE + lax.rem(y + dy + SIDE, SIDE)) * 2 + c, z)

    def along(d):
        return (s, lax.rem(z + d + groups, groups))

    def slot(dx, dy):
        return (lax.rem(x + dx + SIDE, SIDE) * SIDE + lax.rem(y + dy + SIDE, SIDE)) * 2 + core

    def copy(src, dst, ssem, rsem, to):
        return pltpu.make_async_remote_copy(
            src_ref=src, dst_ref=dst, send_sem=ssem, recv_sem=rsem, device_id=to, device_id_type=MESH
        )

    sent = []

    def send(src, dst, ssem, rsem, to):
        c = copy(src, dst, ssem, rsem, to)
        c.start()
        sent.append(c)

    def arrived(ref, rsem):
        copy(ref, ref, rsem, rsem, along(1)).wait_recv()

    barrier = pltpu.get_barrier_semaphore()
    near = [along(1), along(-1), at(1, 0), at(-1, 0), at(0, 1), at(0, -1), at(0, 0, 1)]
    for to in near:
        pl.semaphore_signal(barrier, inc=1, device_id=to, device_id_type=MESH)
    pl.semaphore_wait(barrier, len(near))

    def part_of(ref, q):
        return ref.at[pl.ds(q * n, n)]

    right_order = tuple(range(PIECES))
    left_order = right_order[PIECES // 2:] + right_order[:PIECES // 2]

    def halfway(q, forward):
        return (q < PIECES // 2) == forward

    def ring_send(t, q, forward):
        hop = 1 if forward else -1
        k = lax.rem(z - hop * t + groups, groups)
        src = part_of(feat, q) if t == 0 else part_of(fs.at[k], q)
        i = 0 if forward else 1
        send(src, part_of(fs.at[k], q), ag_send.at[i, t, q], ag_recv.at[i, t, q], along(hop))

    def ring_wait(t, q, forward):
        hop = 1 if forward else -1
        k = lax.rem(z - hop * (t + 1) + groups, groups)
        arrived(part_of(fs.at[k], q), ag_recv.at[0 if forward else 1, t, q])

    def ring_step(t, pieces=range(PIECES)):
        for p in pieces:
            for forward, q in ((True, right_order[p]), (False, left_order[p])):
                ring_wait(t - 1, q, forward)
                if t < far - 1 or halfway(q, forward):
                    ring_send(t, q, forward)

    x_off = (0, -1, 1, 2)
    own = 2 * chip + core

    def to_y(j, src):
        k = slot(x_off[j], 0)
        send(src, hs.at[k], hy_send.at[j, 0], hy_recv.at[j, 0], at(0, 1))
        send(src, hs.at[k], hy_send.at[j, 1], hy_recv.at[j, 1], at(0, -1))

    def to_core(j, i, src):
        k = slot(x_off[j], x_off[i])
        send(src, hs.at[k], hc_send.at[j, i], hc_recv.at[j, i], at(0, 0, 1))

    for p in range(PIECES):
        ring_send(0, right_order[p], True)
        ring_send(0, left_order[p], False)
    send(head, hs.at[own], hx_send.at[0], hx_recv.at[0], at(1, 0))
    send(head, hs.at[own], hx_send.at[1], hx_recv.at[1], at(-1, 0))
    to_y(0, head)
    to_core(0, 0, head)
    mine = [
        pltpu.make_async_copy(feat, fs.at[z], local.at[0]),
        pltpu.make_async_copy(head, hs.at[own], local.at[1]),
        pltpu.make_async_copy(cap_in, cap, local.at[2]),
    ]
    for c in mine:
        c.start()

    def x_near():
        behind = slot(-way, 0)
        arrived(hs.at[behind], hx_recv.at[core])
        send(hs.at[behind], hs.at[behind], hx_send.at[2], hx_recv.at[2], at(way, 0))
        arrived(hs.at[slot(way, 0)], hx_recv.at[1 - core])
        for j in (1, 2):
            to_y(j, hs.at[slot(x_off[j], 0)])
            to_core(j, 0, hs.at[slot(x_off[j], 0)])

    def x_far():
        arrived(hs.at[slot(2, 0)], hx_recv.at[2])
        to_y(3, hs.at[slot(2, 0)])
        to_core(3, 0, hs.at[slot(2, 0)])

    def y_pair(j):
        k = slot(x_off[j], -way)
        arrived(hs.at[k], hy_recv.at[j, core])
        send(hs.at[k], hs.at[k], hy_send.at[j, 2], hy_recv.at[j, 2], at(0, way))
        arrived(hs.at[slot(x_off[j], way)], hy_recv.at[j, 1 - core])
        to_core(j, 1, hs.at[slot(x_off[j], -1)])
        to_core(j, 2, hs.at[slot(x_off[j], 1)])

    def y_far(j):
        k = slot(x_off[j], 2)
        arrived(hs.at[k], hy_recv.at[j, 2])
        to_core(j, 3, hs.at[k])

    x_near()
    ring_step(1)
    y_pair(0)
    ring_step(2, range(PIECES // 2))
    x_far()
    ring_step(2, range(PIECES // 2, PIECES))
    y_far(0)
    y_pair(1)
    ring_step(3, range(PIECES // 2))
    y_pair(2)
    ring_step(3, range(PIECES // 2, PIECES))
    y_far(1)
    y_pair(3)
    ring_step(4, range(PIECES // 2))
    y_far(2)
    ring_step(4, range(PIECES // 2, PIECES))
    y_far(3)
    ring_step(5)

    def head_of(k):
        return hs[pl.ds(2 * k, 2)].reshape(slab, classes)

    def logits_of(slots, r0, count):
        left = jnp.concatenate([fs[k, pl.ds(r0, count), :] for k in slots], axis=1)
        right = jnp.concatenate([head_of(k) for k in slots], axis=0)
        return jnp.dot(left, right, preferred_element_type=F32)

    def around(*distances):
        return [lax.rem(z + d, groups) for e in distances for d in (groups - e, e)]

    ring_step(6)
    for j in range(4):
        for i in range(4):
            k = (lax.rem(x + x_off[j] + SIDE, SIDE) * SIDE + lax.rem(y + x_off[i] + SIDE, SIDE)) * 2 + (1 - core)
            arrived(hs.at[k], hc_recv.at[j, i])
    for c in mine:
        c.wait()
    acc[...] = logits_of(around(1, 2), 0, rows)
    acc[...] += logits_of(around(3, 4), 0, rows)
    ring_step(7, range(PIECES // 2))
    acc[...] += logits_of(around(5, 6), 0, rows)
    ring_step(7, range(PIECES // 2, PIECES))
    acc[...] += logits_of(around(7), 0, rows)

    lanes = 128
    tiles = classes // lanes

    def lane_tiles(v):
        return [v[:, i * lanes:(i + 1) * lanes] for i in range(tiles)]

    def turned_sum(v):
        return jnp.sum(sum(lane_tiles(v)[1:], lane_tiles(v)[0]).T, axis=0, keepdims=True)

    opposite = lax.rem(z + far, groups)
    start_order = [q for pair in zip(right_order[: PIECES // 2], left_order[: PIECES // 2]) for q in pair]
    for q in start_order:
        ring_wait(far - 1, q, halfway(q, True))
        r0 = q * n
        block = pl.ds(r0, n)
        tanh = jnp.tanh((acc[block, :] + logits_of([z, opposite], r0, n)) / softcap)
        student = jnp.exp(softcap * tanh)
        transport = student * student
        stu[block, :] = student
        plan[block, :] = transport
        slope[block, :] = 1.0 - tanh * tanh
        zs0[:, r0:r0 + n] = turned_sum(transport)
        zs0[:, rows + r0:rows + r0 + n] = turned_sum(student)

    z_order = sorted(range(1, groups), key=lambda d: -min(d, groups - d))

    def z_exchange(mine, theirs, i):
        for d in z_order:
            copy(mine, theirs.at[d - 1], zsend.at[i], zrecv.at[i], along(d)).start()

    def z_total(mine, theirs, i):
        copy(theirs, theirs, zsend.at[i], zrecv.at[i], along(1)).wait_recv()
        return mine[...] + jnp.sum(theirs[...], axis=0)

    def c_exchange(mine, theirs, i):
        for n, (dx, dy, dc) in enumerate(OTHERS):
            copy(mine, theirs.at[n], csend.at[i], crecv.at[i], at(dx, dy, dc)).start()

    def c_total(mine, theirs, i):
        copy(theirs, theirs, csend.at[i], crecv.at[i], along(1)).wait_recv()
        return mine[...] + jnp.sum(theirs[...], axis=0)

    def upright(row, r0):
        return jnp.broadcast_to(row[:, r0:r0 + lanes], (lanes, lanes)).T

    z_exchange(zs0, zr0, 0)

    def turn(k, carry):
        t = fs[k].T
        for c in range(2):
            fta[c, lax.rem(k, SIDE), k // SIDE] = t[(2 * c) * quarter:(2 * c + 1) * quarter]
            ftb[c, k // SIDE, lax.rem(k, SIDE)] = t[(2 * c + 1) * quarter:(2 * c + 2) * quarter]
        ht[k] = head_of(k).T
        return carry

    lax.fori_loop(0, groups, turn, 0)

    ceiling = cap[...].astype(F32).reshape(1, classes) * ratio
    scale = jnp.ones((1, classes), F32)
    both = z_total(zs0, zr0, 0)
    mass = both[:, :rows]
    student_mass = both[:, rows:]
    for it in range(ITERS):
        inverse = 1.0 / mass
        column = jnp.zeros((1, classes), F32)
        for r0 in range(0, rows, lanes):
            up = upright(inverse, r0)
            rep = jnp.concatenate([up] * tiles, axis=1)
            column += jnp.sum(plan[pl.ds(r0, lanes), :] * rep, axis=0, keepdims=True)
        cs[it] = column
        c_exchange(cs.at[it], cr.at[it], it)
        total = c_total(cs.at[it], cr.at[it], it)
        scale = jnp.minimum(scale, ceiling / total)
        for r0 in range(0, rows, lanes):
            zs[it, :, r0:r0 + lanes] = turned_sum(plan[pl.ds(r0, lanes), :] * scale)
        z_exchange(zs.at[it], zr.at[it], it + 1)
        mass = z_total(zs.at[it], zr.at[it], it + 1)

    def rs_send_to(d, q, right):
        i = 0 if right else 1
        src = part.at[d if right or d == far else groups - d]
        dst = from_l if right else from_r
        send(part_of(src, q), part_of(dst.at[d - 1], q), rs_send.at[i, d - 1, q], rs_recv.at[i, d - 1, q],
             along(1 if right else -1))

    def rs_add(d, q, right):
        i = 0 if right else 1
        got = (from_l if right else from_r).at[d]
        mine = part.at[d if right else groups - d]
        arrived(part_of(got, q), rs_recv.at[i, d, q])
        block = pl.ds(q * n, n)
        mine[block, :] = (mine[block, :].astype(F32) + got[block, :].astype(F32)).astype(BF)
        rs_send_to(d, q, right)

    rs_events = [(far - 1, right_order[p], left_order[p]) for p in range(PIECES // 2)]
    rs_events += [(d, left_order[p], right_order[p]) for d in range(far - 2, 0, -1) for p in range(PIECES)]

    def share_pair(d, r0=0, count=rows):
        right = lax.rem(z + d, groups)
        left = lax.rem(z - d + groups, groups) if d < far else z
        both = jnp.concatenate([ht[right], ht[left]], axis=1)
        block = pl.ds(r0, count)
        out = jnp.dot(grad[block, :], both, preferred_element_type=F32).astype(BF)
        part[d, block, :] = out[:, :slab]
        part[groups - d if d < far else 0, block, :] = out[:, slab:]

    inverse = 1.0 / mass
    student_inverse = 1.0 / student_mass
    for q in start_order:
        r0 = q * n
        block = pl.ds(r0, n)
        up = jnp.concatenate([upright(inverse, r0)] * tiles, axis=1)
        sup = jnp.concatenate([upright(student_inverse, r0)] * tiles, axis=1)
        targets = (plan[block, :] * up * scale).astype(BF)
        tgt[block, :] = targets
        grad[block, :] = ((stu[block, :] * sup - targets.astype(F32)) * slope[block, :]).astype(BF)
        share_pair(far, r0, n)
        rs_send_to(far, q, halfway(q, True))

    share_pair(far - 1)
    for p in range(PIECES // 2):
        rs_send_to(far - 1, left_order[p], True)
        rs_send_to(far - 1, right_order[p], False)

    def summed(*refs):
        out = refs[0].astype(F32)
        for r in refs[1:]:
            out = out + r.astype(F32)
        return out.astype(BF)

    fwd = 1 + 2 * core
    bwd = 3 - 2 * core

    def first_to(half, d):
        return at(d, 0) if half else at(0, d)

    def second_to(half, d):
        return at(0, d) if half else at(d, 0)

    def first_pos(half, d):
        return lax.rem((x if half else y) + d + SIDE, SIDE)

    def second_pos(half, d):
        return lax.rem((y if half else x) + d + SIDE, SIDE)

    def head_share(out, half, c, pair):
        turned = ftb if half else fta
        lhs = jnp.concatenate([turned[c, first_pos(half, i)].reshape(SIDE * quarter, rows) for i in pair], axis=0)
        share = jnp.dot(lhs, grad[...], preferred_element_type=F32).astype(BF)
        for n_, i in enumerate(pair):
            out[half, i] = share[n_ * SIDE * quarter:(n_ + 1) * SIDE * quarter].reshape(SIDE, quarter, classes)

    def give(half, pair):
        head_share(qo, half, 1 - core, pair)
        for i in pair:
            send(qo.at[half, i], core_in.at[half, i], qc_send.at[half, i], qc_recv.at[half, i], at(0, 0, 1))

    def keep(half):
        head_share(qa, half, core, (2, 1))
        head_share(qa, half, core, (3, 0))

    def chip_sum(half):
        for i in (2, 1, 3, 0):
            arrived(core_in.at[half, i], qc_recv.at[half, i])
            qa[half, i] = summed(qa[half, i], core_in[half, i])
            if i == 2:
                send(qa.at[half, 2], first_in.at[half, 0], q1_send.at[half, 0], q1_recv.at[half, 0], first_to(half, way))
            if i == 3:
                send(qa.at[half, bwd], first_in.at[half, 1], q1_send.at[half, 1], q1_recv.at[half, 1],
                     first_to(half, -way))

    def first_mid(half):
        arrived(first_in.at[half, 0], q1_recv.at[half, 0])
        qa[half, fwd] = summed(qa[half, fwd], first_in[half, 0])
        send(qa.at[half, fwd], first_in.at[half, 2], q1_send.at[half, 2], q1_recv.at[half, 2], first_to(half, way))

    def first_end(half):
        arrived(first_in.at[half, 1], q1_recv.at[half, 1])
        arrived(first_in.at[half, 2], q1_recv.at[half, 2])
        qb[half] = summed(qa[half, 0], first_in[half, 1], first_in[half, 2])
        send(qb.at[half, second_pos(half, 2)], second_in.at[half, 0], q2_send.at[half, 0], q2_recv.at[half, 0],
             second_to(half, way))
        send(qb.at[half, second_pos(half, -way)], second_in.at[half, 1], q2_send.at[half, 1], q2_recv.at[half, 1],
             second_to(half, -way))

    def second_mid(half):
        arrived(second_in.at[half, 0], q2_recv.at[half, 0])
        k = second_pos(half, way)
        qb[half, k] = summed(qb[half, k], second_in[half, 0])
        send(qb.at[half, k], second_in.at[half, 2], q2_send.at[half, 2], q2_recv.at[half, 2], second_to(half, way))

    def second_end(half):
        arrived(second_in.at[half, 1], q2_recv.at[half, 1])
        arrived(second_in.at[half, 2], q2_recv.at[half, 2])
        total = summed(qb[half, second_pos(half, 0)], second_in[half, 1], second_in[half, 2])
        ghead[half * quarter:(half + 1) * quarter, :] = total

    give(0, (2, 1))
    give(0, (3, 0))
    share_pair(6)
    between = {
        0: [(give, 1, (2, 1))], 1: [(give, 1, (3, 0))], 2: [(keep, 0)], 3: [(share_pair, 5)], 4: [(keep, 1), (chip_sum, 0)],
        5: [(chip_sum, 1)], 6: [(share_pair, 4)], 7: [(share_pair, 3)], 8: [(share_pair, 2)], 9: [(share_pair, 1)],
        11: [(first_mid, 0)], 12: [(first_mid, 1)], 16: [(first_end, 0)], 17: [(first_end, 1)],
        20: [(second_mid, 0)], 21: [(second_mid, 1)], 25: [(second_end, 0), (second_end, 1)],
    }
    for e, (d, to_right, to_left) in enumerate(rs_events):
        rs_add(d, to_right, True)
        rs_add(d, to_left, False)
        for task, *what in between.get(e, ()):
            task(*what)

    for p in range(PIECES):
        arrived(part_of(from_l.at[0], left_order[p]), rs_recv.at[0, 0, left_order[p]])
        arrived(part_of(from_r.at[0], right_order[p]), rs_recv.at[1, 0, right_order[p]])
    gfeat[...] = summed(part[0], from_l[0], from_r[0])

    copy(zr0, zr0, zsend.at[0], zrecv.at[0], along(1)).wait_send()
    for it in range(ITERS):
        copy(zr.at[it], zr.at[it], zsend.at[it + 1], zrecv.at[it + 1], along(1)).wait_send()
        copy(cr.at[it], cr.at[it], csend.at[it], crecv.at[it], along(1)).wait_send()
    for c in sent:
        c.wait_send()


def store_kernel(*refs):
    count = len(refs) // 2
    copies = [pltpu.make_async_copy(refs[i], refs[count + i], refs[-1].at[i]) for i in range(count)]
    for c in copies:
        c.start()
    for c in copies:
        c.wait()


def store(results):
    return pl.pallas_call(
        store_kernel,
        out_shape=tuple(jax.ShapeDtypeStruct(r.shape, r.dtype) for r in results),
        in_specs=[pl.BlockSpec(memory_space=pltpu.VMEM)] * len(results),
        out_specs=(pl.BlockSpec(memory_space=pltpu.HBM),) * len(results),
        scratch_shapes=[pltpu.SemaphoreType.DMA((len(results),))],
        compiler_params=pltpu.CompilerParams(vmem_limit_bytes=4 << 20),
    )(*results)


def solution(mesh):
    groups = mesh.shape["cls"]
    samples = mesh.shape["sample"]

    def per_device(features, head, class_cap):
        rows, slab = features.shape
        depth, classes = head.shape
        width = slab * groups
        chips = samples // 2
        far = groups // 2
        ratio = rows * samples / (classes * groups)
        V = pltpu.VMEM
        dma = pltpu.SemaphoreType.DMA
        scratch = [
            V((groups, rows, slab), BF), V((samples, depth, classes), BF),
            V((2, SIDE, SIDE, depth // 2, rows), BF), V((2, SIDE, SIDE, depth // 2, rows), BF), V((groups, classes, slab), BF),
            V((rows, classes), F32), V((rows, classes), F32), V((rows, classes), F32), V((rows, classes), F32),
            V((rows, classes), BF),
            V((groups, rows, slab), BF), V((far, rows, slab), BF), V((far, rows, slab), BF),
            V((2, SIDE, SIDE, depth // 2, classes), BF), V((2, SIDE, SIDE, depth // 2, classes), BF),
            V((2, SIDE, SIDE, depth // 2, classes), BF), V((2, 3, SIDE, depth // 2, classes), BF),
            V((2, SIDE, depth // 2, classes), BF), V((2, 3, depth // 2, classes), BF),
            V((1, 2 * rows), F32), V((ITERS, 1, rows), F32),
            V((groups - 1, 1, 2 * rows), F32), V((ITERS, groups - 1, 1, rows), F32),
            V((ITERS, 1, classes), F32), V((ITERS, samples - 1, 1, classes), F32),
            dma((2, far, PIECES)), dma((2, far, PIECES)), dma((3,)), dma((3,)), dma((4, 3)), dma((4, 3)), dma((4, 4)), dma((4, 4)),
            dma((ITERS + 1,)), dma((ITERS + 1,)), dma((ITERS,)), dma((ITERS,)),
            V((classes,), BF), dma((3,)),
            dma((2, far, PIECES)), dma((2, far, PIECES)), dma((2, 4)), dma((2, 4)), dma((2, 3)), dma((2, 3)), dma((2, 3)), dma((2, 3)),
        ]
        vmem = pl.BlockSpec(memory_space=pltpu.VMEM)
        hbm = pl.BlockSpec(memory_space=pltpu.HBM)
        results = pl.pallas_call(
            functools.partial(kernel, rows, width, classes, groups, ratio),
            out_shape=(
                jax.ShapeDtypeStruct((rows, classes), BF),
                jax.ShapeDtypeStruct((rows, slab), BF),
                jax.ShapeDtypeStruct((depth, classes), BF),
            ),
            in_specs=[hbm] * 3,
            out_specs=(vmem,) * 3,
            scratch_shapes=scratch,
            compiler_params=pltpu.CompilerParams(
                collective_id=0, has_side_effects=True, vmem_limit_bytes=48 << 20
            ),
        )(*(pltpu.with_memory_space_constraint(a, pltpu.HBM) for a in (features, head, class_cap)))
        return store(results)

    return jax.shard_map(
        per_device,
        mesh=mesh,
        in_specs=(P("sample", "cls"), P("sample", "cls"), P("cls")),
        out_specs=(P("sample", "cls"), P("sample", "cls"), P("sample", "cls")),
        check_vma=False,
    )
```

```python
import functools
import jax
import jax.numpy as jnp
from jax import lax
from jax.experimental import pallas as pl
from jax.experimental.pallas import tpu as pltpu
from jax.sharding import PartitionSpec as P

ITERS = 3
softcap = 15.0
sharpen = 2.0
MESH = pl.DeviceIdType.MESH
SIDE = 4
PIECES = 4
BF = jnp.bfloat16
F32 = jnp.float32

OTHERS = sorted(
    ((dx, dy, dc) for dx in range(SIDE) for dy in range(SIDE) for dc in range(2) if dx or dy or dc),
    key=lambda o: -(min(o[0], SIDE - o[0]) + min(o[1], SIDE - o[1]) + 0.5 * o[2]),
)


def kernel(
    rows, width, classes, groups, ratio,
    feat, head, cap_in,
    tgt, gfeat, ghead,
    fs, hs, fta, ftb, ht, acc, stu, plan, slope, grad,
    part, from_l, from_r,
    split, early, early_in, late,
    qo, core_in, qa, first_in, qb, second_in,
    zs0, zs, zr0, zr, cs, cr,
    ag_send, ag_recv, hx_send, hx_recv, hy_send, hy_recv, hc_send, hc_recv,
    zsend, zrecv, csend, crecv, cap, local, e_send, e_recv,
    rs_send, rs_recv, qc_send, qc_recv, q1_send, q1_recv, q2_send, q2_recv,
):
    s = lax.axis_index("sample")
    z = lax.axis_index("cls")
    core = lax.rem(s, 2)
    chip = s // 2
    y = lax.rem(chip, SIDE)
    x = chip // SIDE
    way = 1 - 2 * core
    n = rows // PIECES
    slab = width // groups
    far = groups // 2
    quarter = slab // 4

    def at(dx, dy, flip=0):
        c = lax.rem(core + flip, 2)
        return ((lax.rem(x + dx + SIDE, SIDE) * SIDE + lax.rem(y + dy + SIDE, SIDE)) * 2 + c, z)

    def along(d):
        return (s, lax.rem(z + d + groups, groups))

    def slot(dx, dy):
        return (lax.rem(x + dx + SIDE, SIDE) * SIDE + lax.rem(y + dy + SIDE, SIDE)) * 2 + core

    def copy(src, dst, ssem, rsem, to):
        return pltpu.make_async_remote_copy(
            src_ref=src, dst_ref=dst, send_sem=ssem, recv_sem=rsem, device_id=to, device_id_type=MESH
        )

    sent = []

    def send(src, dst, ssem, rsem, to):
        c = copy(src, dst, ssem, rsem, to)
        c.start()
        sent.append(c)

    def arrived(ref, rsem):
        copy(ref, ref, rsem, rsem, along(1)).wait_recv()

    barrier = pltpu.get_barrier_semaphore()
    near = [along(1), along(-1), at(1, 0), at(-1, 0), at(0, 1), at(0, -1), at(0, 0, 1)]
    for to in near:
        pl.semaphore_signal(barrier, inc=1, device_id=to, device_id_type=MESH)
    pl.semaphore_wait(barrier, len(near))

    def part_of(ref, q):
        return ref.at[pl.ds(q * n, n)]

    right_order = tuple(range(PIECES))
    left_order = right_order[PIECES // 2:] + right_order[:PIECES // 2]

    def halfway(q, forward):
        return (q < PIECES // 2) == forward

    def ring_send(t, q, forward):
        hop = 1 if forward else -1
        k = lax.rem(z - hop * t + groups, groups)
        src = part_of(feat, q) if t == 0 else part_of(fs.at[k], q)
        i = 0 if forward else 1
        send(src, part_of(fs.at[k], q), ag_send.at[i, t, q], ag_recv.at[i, t, q], along(hop))

    def ring_wait(t, q, forward):
        hop = 1 if forward else -1
        k = lax.rem(z - hop * (t + 1) + groups, groups)
        arrived(part_of(fs.at[k], q), ag_recv.at[0 if forward else 1, t, q])

    def ring_step(t, pieces=range(PIECES)):
        for p in pieces:
            for forward, q in ((True, right_order[p]), (False, left_order[p])):
                ring_wait(t - 1, q, forward)
                if t < far - 1 or halfway(q, forward):
                    ring_send(t, q, forward)

    x_off = (0, -1, 1, 2)
    own = 2 * chip + core

    def to_y(j, src):
        k = slot(x_off[j], 0)
        send(src, hs.at[k], hy_send.at[j, 0], hy_recv.at[j, 0], at(0, 1))
        send(src, hs.at[k], hy_send.at[j, 1], hy_recv.at[j, 1], at(0, -1))

    def to_core(j, i, src):
        k = slot(x_off[j], x_off[i])
        send(src, hs.at[k], hc_send.at[j, i], hc_recv.at[j, i], at(0, 0, 1))

    for p in range(PIECES):
        ring_send(0, right_order[p], True)
        ring_send(0, left_order[p], False)
    send(head, hs.at[own], hx_send.at[0], hx_recv.at[0], at(1, 0))
    send(head, hs.at[own], hx_send.at[1], hx_recv.at[1], at(-1, 0))
    to_y(0, head)
    to_core(0, 0, head)
    mine = [
        pltpu.make_async_copy(feat, fs.at[z], local.at[0]),
        pltpu.make_async_copy(head, hs.at[own], local.at[1]),
        pltpu.make_async_copy(cap_in, cap, local.at[2]),
    ]
    for c in mine:
        c.start()

    def x_near():
        behind = slot(-way, 0)
        arrived(hs.at[behind], hx_recv.at[core])
        send(hs.at[behind], hs.at[behind], hx_send.at[2], hx_recv.at[2], at(way, 0))
        arrived(hs.at[slot(way, 0)], hx_recv.at[1 - core])
        for j in (1, 2):
            to_y(j, hs.at[slot(x_off[j], 0)])
            to_core(j, 0, hs.at[slot(x_off[j], 0)])

    def x_far():
        arrived(hs.at[slot(2, 0)], hx_recv.at[2])
        to_y(3, hs.at[slot(2, 0)])
        to_core(3, 0, hs.at[slot(2, 0)])

    def y_pair(j):
        k = slot(x_off[j], -way)
        arrived(hs.at[k], hy_recv.at[j, core])
        send(hs.at[k], hs.at[k], hy_send.at[j, 2], hy_recv.at[j, 2], at(0, way))
        arrived(hs.at[slot(x_off[j], way)], hy_recv.at[j, 1 - core])
        to_core(j, 1, hs.at[slot(x_off[j], -1)])
        to_core(j, 2, hs.at[slot(x_off[j], 1)])

    def y_far(j):
        k = slot(x_off[j], 2)
        arrived(hs.at[k], hy_recv.at[j, 2])
        to_core(j, 3, hs.at[k])

    x_near()
    ring_step(1)
    y_pair(0)
    ring_step(2, range(PIECES // 2))
    x_far()
    ring_step(2, range(PIECES // 2, PIECES))
    y_far(0)
    y_pair(1)
    ring_step(3, range(PIECES // 2))
    y_pair(2)
    ring_step(3, range(PIECES // 2, PIECES))
    y_far(1)
    y_pair(3)
    ring_step(4, range(PIECES // 2))
    y_far(2)
    ring_step(4, range(PIECES // 2, PIECES))
    y_far(3)
    ring_step(5)

    def head_of(k):
        return hs[pl.ds(2 * k, 2)].reshape(slab, classes)

    def logits_of(slots, r0, count):
        left = jnp.concatenate([fs[k, pl.ds(r0, count), :] for k in slots], axis=1)
        right = jnp.concatenate([head_of(k) for k in slots], axis=0)
        return jnp.dot(left, right, preferred_element_type=F32)

    def around(*distances):
        return [lax.rem(z + d, groups) for e in distances for d in (groups - e, e)]

    ring_step(6)
    for j in range(4):
        for i in range(4):
            k = (lax.rem(x + x_off[j] + SIDE, SIDE) * SIDE + lax.rem(y + x_off[i] + SIDE, SIDE)) * 2 + (1 - core)
            arrived(hs.at[k], hc_recv.at[j, i])
    for c in mine:
        c.wait()
    acc[...] = logits_of(around(1, 2), 0, rows)
    acc[...] += logits_of(around(3, 4), 0, rows)
    ring_step(7, range(PIECES // 2))
    acc[...] += logits_of(around(5, 6), 0, rows)
    ring_step(7, range(PIECES // 2, PIECES))
    acc[...] += logits_of(around(7), 0, rows)

    lanes = 128
    tiles = classes // lanes

    def lane_tiles(v):
        return [v[:, i * lanes:(i + 1) * lanes] for i in range(tiles)]

    def turned_sum(v):
        return jnp.sum(sum(lane_tiles(v)[1:], lane_tiles(v)[0]).T, axis=0, keepdims=True)

    opposite = lax.rem(z + far, groups)
    start_order = [q for pair in zip(right_order[: PIECES // 2], left_order[: PIECES // 2]) for q in pair]
    for q in start_order:
        ring_wait(far - 1, q, halfway(q, True))
        r0 = q * n
        block = pl.ds(r0, n)
        tanh = jnp.tanh((acc[block, :] + logits_of([z, opposite], r0, n)) / softcap)
        student = jnp.exp(softcap * tanh)
        transport = student * student
        stu[block, :] = student
        plan[block, :] = transport
        slope[block, :] = 1.0 - tanh * tanh
        zs0[:, r0:r0 + n] = turned_sum(transport)
        zs0[:, rows + r0:rows + r0 + n] = turned_sum(student)

    z_order = sorted(range(1, groups), key=lambda d: -min(d, groups - d))

    def z_exchange(mine, theirs, i):
        for d in z_order:
            copy(mine, theirs.at[d - 1], zsend.at[i], zrecv.at[i], along(d)).start()

    def z_total(mine, theirs, i):
        copy(theirs, theirs, zsend.at[i], zrecv.at[i], along(1)).wait_recv()
        return mine[...] + jnp.sum(theirs[...], axis=0)

    def c_exchange(mine, theirs, i):
        for n, (dx, dy, dc) in enumerate(OTHERS):
            copy(mine, theirs.at[n], csend.at[i], crecv.at[i], at(dx, dy, dc)).start()

    def c_total(mine, theirs, i):
        copy(theirs, theirs, csend.at[i], crecv.at[i], along(1)).wait_recv()
        return mine[...] + jnp.sum(theirs[...], axis=0)

    def upright(row, r0):
        return jnp.broadcast_to(row[:, r0:r0 + lanes], (lanes, lanes)).T

    z_exchange(zs0, zr0, 0)

    def turn(k, carry):
        t = fs[k].T
        for c in range(2):
            fta[c, lax.rem(k, SIDE), k // SIDE] = t[(2 * c) * quarter:(2 * c + 1) * quarter]
            ftb[c, k // SIDE, lax.rem(k, SIDE)] = t[(2 * c + 1) * quarter:(2 * c + 2) * quarter]
        ht[k] = head_of(k).T
        return carry

    lax.fori_loop(0, groups, turn, 0)

    def early_share(w, r0, count):
        block = pl.ds(r0, count)
        early[w, 0, block, :] = jnp.dot(split[w, block, :], ht[opposite], preferred_element_type=F32).astype(BF)

    def pair_share(w, d):
        both = jnp.concatenate([ht[lax.rem(z + d, groups)], ht[lax.rem(z - d + groups, groups)]], axis=1)
        return jnp.dot(split[w], both, preferred_element_type=F32)

    def early_near(w):
        out = pair_share(w, far - 1).astype(BF)
        early[w, 1] = out[:, :slab]
        early[w, 2] = out[:, slab:]

    def early_send(w, level, q, right):
        i = 0 if right else 1
        src = early.at[w, 0 if level == 0 else 1 + i]
        send(part_of(src, q), part_of(early_in.at[w, i, level], q), e_send.at[w, i, level, q],
             e_recv.at[w, i, level, q], along(1 if right else -1))

    def early_wait(w, level, q, right):
        i = 0 if right else 1
        arrived(part_of(early_in.at[w, i, level], q), e_recv.at[w, i, level, q])

    def early_fresh(w):
        for p in range(PIECES // 2):
            early_send(w, 1, left_order[p], True)
            early_send(w, 1, right_order[p], False)

    def early_pass(w):
        for p in range(PIECES // 2):
            for q, right in ((right_order[p], True), (left_order[p], False)):
                i = 0 if right else 1
                early_wait(w, 0, q, right)
                block = pl.ds(q * n, n)
                added = early[w, 1 + i, block, :].astype(F32) + early_in[w, i, 0, block, :].astype(F32)
                early[w, 1 + i, block, :] = added.astype(BF)
                early_send(w, 1, q, right)

    def late_shares(w):
        for m, d in enumerate((far - 2, far - 3)):
            late[w, m] = pair_share(w, d)

    def while_columns_travel(it):
        if it == 0:
            for q in start_order:
                block = pl.ds(q * n, n)
                sup = jnp.concatenate([upright(student_inverse, q * n)] * tiles, axis=1)
                split[0, block, :] = (stu[block, :] * sup * slope[block, :]).astype(BF)
                early_share(0, q * n, n)
                early_send(0, 0, q, halfway(q, True))
            early_near(0)
            early_fresh(0)
        elif it == 1:
            early_pass(0)
        elif it == 2:
            late_shares(0)

    def while_last_rows_travel(scale):
        for q in start_order:
            block = pl.ds(q * n, n)
            split[1, block, :] = (plan[block, :] * scale * slope[block, :]).astype(BF)
            early_share(1, q * n, n)
            early_send(1, 0, q, halfway(q, True))
        early_near(1)
        early_fresh(1)
        late_shares(1)
        early_pass(1)

    ceiling = cap[...].astype(F32).reshape(1, classes) * ratio
    scale = jnp.ones((1, classes), F32)
    both = z_total(zs0, zr0, 0)
    mass = both[:, :rows]
    student_inverse = 1.0 / both[:, rows:]
    for it in range(ITERS):
        inverse = 1.0 / mass
        column = jnp.zeros((1, classes), F32)
        for r0 in range(0, rows, lanes):
            up = upright(inverse, r0)
            rep = jnp.concatenate([up] * tiles, axis=1)
            column += jnp.sum(plan[pl.ds(r0, lanes), :] * rep, axis=0, keepdims=True)
        cs[it] = column
        c_exchange(cs.at[it], cr.at[it], it)
        while_columns_travel(it)
        total = c_total(cs.at[it], cr.at[it], it)
        scale = jnp.minimum(scale, ceiling / total)
        for r0 in range(0, rows, lanes):
            zs[it, :, r0:r0 + lanes] = turned_sum(plan[pl.ds(r0, lanes), :] * scale)
        z_exchange(zs.at[it], zr.at[it], it + 1)
        if it == ITERS - 1:
            while_last_rows_travel(scale)
        mass = z_total(zs.at[it], zr.at[it], it + 1)

    def rs_send_to(d, q, right):
        i = 0 if right else 1
        src = part.at[d if right or d == far else groups - d]
        dst = from_l if right else from_r
        send(part_of(src, q), part_of(dst.at[d - 1], q), rs_send.at[i, d - 1, q], rs_recv.at[i, d - 1, q],
             along(1 if right else -1))

    def rs_add(d, q, right):
        i = 0 if right else 1
        got = (from_l if right else from_r).at[d]
        mine = part.at[d if right else groups - d]
        arrived(part_of(got, q), rs_recv.at[i, d, q])
        block = pl.ds(q * n, n)
        mine[block, :] = (mine[block, :].astype(F32) + got[block, :].astype(F32)).astype(BF)
        rs_send_to(d, q, right)

    rs_events = [(d, left_order[p], right_order[p]) for d in range(far - 3, 0, -1) for p in range(PIECES)]

    def share_pair(d):
        both = jnp.concatenate([ht[lax.rem(z + d, groups)], ht[lax.rem(z - d + groups, groups)]], axis=1)
        out = jnp.dot(grad[...], both, preferred_element_type=F32).astype(BF)
        part[d] = out[:, :slab]
        part[groups - d] = out[:, slab:]

    def share_own():
        part[0] = jnp.dot(grad[...], ht[z], preferred_element_type=F32).astype(BF)

    inverse = 1.0 / mass
    ups = [upright(inverse, q * n) for q in range(PIECES)]

    def merge(q, right):
        i = 0 if right else 1
        for w in range(2):
            early_wait(w, 1, q, right)
        block = pl.ds(q * n, n)
        side = slice(i * slab, (i + 1) * slab)
        student_part, plan_part = (late[w, 0, block, side] + early_in[w, i, 1, block, :].astype(F32) for w in range(2))
        part[(far - 2) if right else groups - far + 2, block, :] = (student_part - ups[q] * plan_part).astype(BF)
        rs_send_to(far - 2, q, right)

    for p in range(PIECES // 2):
        merge(left_order[p], True)
        merge(right_order[p], False)
    for q in range(PIECES):
        block = pl.ds(q * n, n)
        up = jnp.concatenate([ups[q]] * tiles, axis=1)
        targets = (plan[block, :] * up * scale).astype(BF)
        tgt[block, :] = targets
        sup = jnp.concatenate([upright(student_inverse, q * n)] * tiles, axis=1)
        grad[block, :] = ((stu[block, :] * sup - targets.astype(F32)) * slope[block, :]).astype(BF)

    def next_shares():
        for q in range(PIECES):
            block = pl.ds(q * n, n)
            both = late[0, 1, block, :] - jnp.concatenate([ups[q]] * 2, axis=1) * late[1, 1, block, :]
            part[far - 3, block, :] = both[:, :slab].astype(BF)
            part[groups - far + 3, block, :] = both[:, slab:].astype(BF)

    def summed(*refs):
        out = refs[0].astype(F32)
        for r in refs[1:]:
            out = out + r.astype(F32)
        return out.astype(BF)

    fwd = 1 + 2 * core
    bwd = 3 - 2 * core

    def first_to(half, d):
        return at(d, 0) if half else at(0, d)

    def second_to(half, d):
        return at(0, d) if half else at(d, 0)

    def first_pos(half, d):
        return lax.rem((x if half else y) + d + SIDE, SIDE)

    def second_pos(half, d):
        return lax.rem((y if half else x) + d + SIDE, SIDE)

    def head_share(out, half, c, pair):
        turned = ftb if half else fta
        lhs = jnp.concatenate([turned[c, first_pos(half, i)].reshape(SIDE * quarter, rows) for i in pair], axis=0)
        share = jnp.dot(lhs, grad[...], preferred_element_type=F32).astype(BF)
        for n_, i in enumerate(pair):
            out[half, i] = share[n_ * SIDE * quarter:(n_ + 1) * SIDE * quarter].reshape(SIDE, quarter, classes)

    def give(half, pair):
        head_share(qo, half, 1 - core, pair)
        for i in pair:
            send(qo.at[half, i], core_in.at[half, i], qc_send.at[half, i], qc_recv.at[half, i], at(0, 0, 1))

    def keep(half):
        head_share(qa, half, core, (2, 1))
        head_share(qa, half, core, (3, 0))

    def chip_sum(half):
        for i in (2, 1, 3, 0):
            arrived(core_in.at[half, i], qc_recv.at[half, i])
            qa[half, i] = summed(qa[half, i], core_in[half, i])
            if i == 2:
                send(qa.at[half, 2], first_in.at[half, 0], q1_send.at[half, 0], q1_recv.at[half, 0], first_to(half, way))
            if i == 3:
                send(qa.at[half, bwd], first_in.at[half, 1], q1_send.at[half, 1], q1_recv.at[half, 1],
                     first_to(half, -way))

    def first_mid(half):
        arrived(first_in.at[half, 0], q1_recv.at[half, 0])
        qa[half, fwd] = summed(qa[half, fwd], first_in[half, 0])
        send(qa.at[half, fwd], first_in.at[half, 2], q1_send.at[half, 2], q1_recv.at[half, 2], first_to(half, way))

    def first_end(half):
        arrived(first_in.at[half, 1], q1_recv.at[half, 1])
        arrived(first_in.at[half, 2], q1_recv.at[half, 2])
        qb[half] = summed(qa[half, 0], first_in[half, 1], first_in[half, 2])
        send(qb.at[half, second_pos(half, 2)], second_in.at[half, 0], q2_send.at[half, 0], q2_recv.at[half, 0],
             second_to(half, way))
        send(qb.at[half, second_pos(half, -way)], second_in.at[half, 1], q2_send.at[half, 1], q2_recv.at[half, 1],
             second_to(half, -way))

    def second_mid(half):
        arrived(second_in.at[half, 0], q2_recv.at[half, 0])
        k = second_pos(half, way)
        qb[half, k] = summed(qb[half, k], second_in[half, 0])
        send(qb.at[half, k], second_in.at[half, 2], q2_send.at[half, 2], q2_recv.at[half, 2], second_to(half, way))

    def second_end(half):
        arrived(second_in.at[half, 1], q2_recv.at[half, 1])
        arrived(second_in.at[half, 2], q2_recv.at[half, 2])
        total = summed(qb[half, second_pos(half, 0)], second_in[half, 1], second_in[half, 2])
        ghead[half * quarter:(half + 1) * quarter, :] = total

    give(0, (2, 1))
    give(0, (3, 0))
    give(1, (2, 1))
    give(1, (3, 0))
    for p in range(PIECES // 2, PIECES):
        merge(left_order[p], True)
        merge(right_order[p], False)
    keep(0)
    next_shares()
    between = {
        0: [(keep, 1)], 1: [(chip_sum, 0)], 2: [(share_pair, 4), (chip_sum, 1)], 3: [(share_pair, 3)], 5: [(share_pair, 2)],
        6: [(share_pair, 1)], 7: [(share_own,)], 8: [(first_mid, 0)], 9: [(first_mid, 1)],
        13: [(first_end, 0)], 14: [(first_end, 1)], 17: [(second_mid, 0)], 18: [(second_mid, 1)],
    }
    for e, (d, to_right, to_left) in enumerate(rs_events):
        rs_add(d, to_right, True)
        rs_add(d, to_left, False)
        for task, *what in between.get(e, ()):
            task(*what)

    for p in range(PIECES):
        arrived(part_of(from_l.at[0], left_order[p]), rs_recv.at[0, 0, left_order[p]])
        arrived(part_of(from_r.at[0], right_order[p]), rs_recv.at[1, 0, right_order[p]])
    second_end(0)
    second_end(1)
    gfeat[...] = summed(part[0], from_l[0], from_r[0])

    copy(zr0, zr0, zsend.at[0], zrecv.at[0], along(1)).wait_send()
    for it in range(ITERS):
        copy(zr.at[it], zr.at[it], zsend.at[it + 1], zrecv.at[it + 1], along(1)).wait_send()
        copy(cr.at[it], cr.at[it], csend.at[it], crecv.at[it], along(1)).wait_send()
    for c in sent:
        c.wait_send()


def store_kernel(*refs):
    count = len(refs) // 2
    copies = [pltpu.make_async_copy(refs[i], refs[count + i], refs[-1].at[i]) for i in range(count)]
    for c in copies:
        c.start()
    for c in copies:
        c.wait()


def store(results):
    return pl.pallas_call(
        store_kernel,
        out_shape=tuple(jax.ShapeDtypeStruct(r.shape, r.dtype) for r in results),
        in_specs=[pl.BlockSpec(memory_space=pltpu.VMEM)] * len(results),
        out_specs=(pl.BlockSpec(memory_space=pltpu.HBM),) * len(results),
        scratch_shapes=[pltpu.SemaphoreType.DMA((len(results),))],
        compiler_params=pltpu.CompilerParams(vmem_limit_bytes=4 << 20),
    )(*results)


def solution(mesh):
    groups = mesh.shape["cls"]
    samples = mesh.shape["sample"]

    def per_device(features, head, class_cap):
        rows, slab = features.shape
        depth, classes = head.shape
        width = slab * groups
        chips = samples // 2
        far = groups // 2
        ratio = rows * samples / (classes * groups)
        V = pltpu.VMEM
        dma = pltpu.SemaphoreType.DMA
        scratch = [
            V((groups, rows, slab), BF), V((samples, depth, classes), BF),
            V((2, SIDE, SIDE, depth // 2, rows), BF), V((2, SIDE, SIDE, depth // 2, rows), BF), V((groups, classes, slab), BF),
            V((rows, classes), F32), V((rows, classes), F32), V((rows, classes), F32), V((rows, classes), F32),
            V((rows, classes), BF),
            V((groups, rows, slab), BF), V((far, rows, slab), BF), V((far, rows, slab), BF),
            V((2, rows, classes), BF), V((2, 3, rows, slab), BF), V((2, 2, 2, rows, slab), BF), V((2, 2, rows, 2 * slab), F32),
            V((2, SIDE, SIDE, depth // 2, classes), BF), V((2, SIDE, SIDE, depth // 2, classes), BF),
            V((2, SIDE, SIDE, depth // 2, classes), BF), V((2, 3, SIDE, depth // 2, classes), BF),
            V((2, SIDE, depth // 2, classes), BF), V((2, 3, depth // 2, classes), BF),
            V((1, 2 * rows), F32), V((ITERS, 1, rows), F32),
            V((groups - 1, 1, 2 * rows), F32), V((ITERS, groups - 1, 1, rows), F32),
            V((ITERS, 1, classes), F32), V((ITERS, samples - 1, 1, classes), F32),
            dma((2, far, PIECES)), dma((2, far, PIECES)), dma((3,)), dma((3,)), dma((4, 3)), dma((4, 3)), dma((4, 4)), dma((4, 4)),
            dma((ITERS + 1,)), dma((ITERS + 1,)), dma((ITERS,)), dma((ITERS,)),
            V((classes,), BF), dma((3,)), dma((2, 2, 2, PIECES)), dma((2, 2, 2, PIECES)),
            dma((2, far, PIECES)), dma((2, far, PIECES)), dma((2, 4)), dma((2, 4)), dma((2, 3)), dma((2, 3)), dma((2, 3)), dma((2, 3)),
        ]
        vmem = pl.BlockSpec(memory_space=pltpu.VMEM)
        hbm = pl.BlockSpec(memory_space=pltpu.HBM)
        results = pl.pallas_call(
            functools.partial(kernel, rows, width, classes, groups, ratio),
            out_shape=(
                jax.ShapeDtypeStruct((rows, classes), BF),
                jax.ShapeDtypeStruct((rows, slab), BF),
                jax.ShapeDtypeStruct((depth, classes), BF),
            ),
            in_specs=[hbm] * 3,
            out_specs=(vmem,) * 3,
            scratch_shapes=scratch,
            compiler_params=pltpu.CompilerParams(
                collective_id=0, has_side_effects=True, vmem_limit_bytes=48 << 20
            ),
        )(*(pltpu.with_memory_space_constraint(a, pltpu.HBM) for a in (features, head, class_cap)))
        return store(results)

    return jax.shard_map(
        per_device,
        mesh=mesh,
        in_specs=(P("sample", "cls"), P("sample", "cls"), P("cls")),
        out_specs=(P("sample", "cls"), P("sample", "cls"), P("sample", "cls")),
        check_vma=False,
    )
```

```python
import functools
import jax
import jax.numpy as jnp
from jax import lax
from jax.experimental import pallas as pl
from jax.experimental.pallas import tpu as pltpu
from jax.sharding import PartitionSpec as P

ITERS = 3
softcap = 15.0
sharpen = 2.0
MESH = pl.DeviceIdType.MESH
SIDE = 4
PIECES = 4
BF = jnp.bfloat16
F32 = jnp.float32

OTHERS = sorted(
    ((dx, dy, dc) for dx in range(SIDE) for dy in range(SIDE) for dc in range(2) if dx or dy or dc),
    key=lambda o: -(min(o[0], SIDE - o[0]) + min(o[1], SIDE - o[1]) + 0.5 * o[2]),
)


def kernel(
    rows, width, classes, groups, ratio,
    feat, head, cap_in,
    tgt, gfeat, ghead,
    fs, hs, fta, ftb, ht, acc, stu, plan, plan_t, slope, grad,
    part, from_l, from_r,
    split, early, early_in, late, beyond,
    qo, core_in, qa, first_in, qb, second_in,
    zs0, zs, zr0, zr, cs, cr,
    ag_send, ag_recv, hx_send, hx_recv, hy_send, hy_recv, hc_send, hc_recv,
    zsend, zrecv, csend, crecv, cap, local, e_send, e_recv,
    rs_send, rs_recv, qc_send, qc_recv, q1_send, q1_recv, q2_send, q2_recv,
):
    s = lax.axis_index("sample")
    z = lax.axis_index("cls")
    core = lax.rem(s, 2)
    chip = s // 2
    y = lax.rem(chip, SIDE)
    x = chip // SIDE
    way = 1 - 2 * core
    n = rows // PIECES
    slab = width // groups
    far = groups // 2
    quarter = slab // 4

    def at(dx, dy, flip=0):
        c = lax.rem(core + flip, 2)
        return ((lax.rem(x + dx + SIDE, SIDE) * SIDE + lax.rem(y + dy + SIDE, SIDE)) * 2 + c, z)

    def along(d):
        return (s, lax.rem(z + d + groups, groups))

    def slot(dx, dy):
        return (lax.rem(x + dx + SIDE, SIDE) * SIDE + lax.rem(y + dy + SIDE, SIDE)) * 2 + core

    def copy(src, dst, ssem, rsem, to):
        return pltpu.make_async_remote_copy(
            src_ref=src, dst_ref=dst, send_sem=ssem, recv_sem=rsem, device_id=to, device_id_type=MESH
        )

    sent = []

    def send(src, dst, ssem, rsem, to):
        c = copy(src, dst, ssem, rsem, to)
        c.start()
        sent.append(c)

    def flush(count):
        for c in sent[:count]:
            c.wait_send()
        del sent[:count]

    def arrived(ref, rsem):
        copy(ref, ref, rsem, rsem, along(1)).wait_recv()

    barrier = pltpu.get_barrier_semaphore()
    near = [along(1), along(-1), at(1, 0), at(-1, 0), at(0, 1), at(0, -1), at(0, 0, 1)]
    for to in near:
        pl.semaphore_signal(barrier, inc=1, device_id=to, device_id_type=MESH)
    pl.semaphore_wait(barrier, len(near))

    def part_of(ref, q):
        return ref.at[pl.ds(q * n, n)]

    right_order = tuple(range(PIECES))
    left_order = right_order[PIECES // 2:] + right_order[:PIECES // 2]

    def halfway(q, forward):
        return (q < PIECES // 2) == forward

    def ring_send(t, q, forward):
        hop = 1 if forward else -1
        k = lax.rem(z - hop * t + groups, groups)
        src = part_of(feat, q) if t == 0 else part_of(fs.at[k], q)
        i = 0 if forward else 1
        send(src, part_of(fs.at[k], q), ag_send.at[i, t, q], ag_recv.at[i, t, q], along(hop))

    def ring_wait(t, q, forward):
        hop = 1 if forward else -1
        k = lax.rem(z - hop * (t + 1) + groups, groups)
        arrived(part_of(fs.at[k], q), ag_recv.at[0 if forward else 1, t, q])

    def ring_step(t, pieces=range(PIECES)):
        for p in pieces:
            for forward, q in ((True, right_order[p]), (False, left_order[p])):
                ring_wait(t - 1, q, forward)
                if t < far - 1 or halfway(q, forward):
                    ring_send(t, q, forward)

    x_off = (0, -1, 1, 2)
    own = 2 * chip + core

    def to_y(j, src):
        k = slot(x_off[j], 0)
        send(src, hs.at[k], hy_send.at[j, 0], hy_recv.at[j, 0], at(0, 1))
        send(src, hs.at[k], hy_send.at[j, 1], hy_recv.at[j, 1], at(0, -1))

    def to_core(j, i, src):
        k = slot(x_off[j], x_off[i])
        send(src, hs.at[k], hc_send.at[j, i], hc_recv.at[j, i], at(0, 0, 1))

    for p in range(PIECES):
        ring_send(0, right_order[p], True)
        ring_send(0, left_order[p], False)
    send(head, hs.at[own], hx_send.at[0], hx_recv.at[0], at(1, 0))
    send(head, hs.at[own], hx_send.at[1], hx_recv.at[1], at(-1, 0))
    to_y(0, head)
    to_core(0, 0, head)
    mine = [
        pltpu.make_async_copy(feat, fs.at[z], local.at[0]),
        pltpu.make_async_copy(head, hs.at[own], local.at[1]),
        pltpu.make_async_copy(cap_in, cap, local.at[2]),
    ]
    for c in mine:
        c.start()

    def x_near():
        behind = slot(-way, 0)
        arrived(hs.at[behind], hx_recv.at[core])
        send(hs.at[behind], hs.at[behind], hx_send.at[2], hx_recv.at[2], at(way, 0))
        arrived(hs.at[slot(way, 0)], hx_recv.at[1 - core])
        for j in (1, 2):
            to_y(j, hs.at[slot(x_off[j], 0)])
            to_core(j, 0, hs.at[slot(x_off[j], 0)])

    def x_far():
        arrived(hs.at[slot(2, 0)], hx_recv.at[2])
        to_y(3, hs.at[slot(2, 0)])
        to_core(3, 0, hs.at[slot(2, 0)])

    def y_pair(j):
        k = slot(x_off[j], -way)
        arrived(hs.at[k], hy_recv.at[j, core])
        send(hs.at[k], hs.at[k], hy_send.at[j, 2], hy_recv.at[j, 2], at(0, way))
        arrived(hs.at[slot(x_off[j], way)], hy_recv.at[j, 1 - core])
        to_core(j, 1, hs.at[slot(x_off[j], -1)])
        to_core(j, 2, hs.at[slot(x_off[j], 1)])

    def y_far(j):
        k = slot(x_off[j], 2)
        arrived(hs.at[k], hy_recv.at[j, 2])
        to_core(j, 3, hs.at[k])

    x_near()
    ring_step(1)
    y_pair(0)
    ring_step(2, range(PIECES // 2))
    x_far()
    ring_step(2, range(PIECES // 2, PIECES))
    y_far(0)
    y_pair(1)
    ring_step(3, range(PIECES // 2))
    y_pair(2)
    ring_step(3, range(PIECES // 2, PIECES))
    y_far(1)
    y_pair(3)
    ring_step(4, range(PIECES // 2))
    y_far(2)
    ring_step(4, range(PIECES // 2, PIECES))
    y_far(3)
    ring_step(5)

    def head_of(k):
        return hs[pl.ds(2 * k, 2)].reshape(slab, classes)

    def logits_of(slots, r0, count):
        left = jnp.concatenate([fs[k, pl.ds(r0, count), :] for k in slots], axis=1)
        right = jnp.concatenate([head_of(k) for k in slots], axis=0)
        return jnp.dot(left, right, preferred_element_type=F32)

    def around(*distances):
        return [lax.rem(z + d, groups) for e in distances for d in (groups - e, e)]

    ring_step(6)
    for j in range(4):
        for i in range(4):
            k = (lax.rem(x + x_off[j] + SIDE, SIDE) * SIDE + lax.rem(y + x_off[i] + SIDE, SIDE)) * 2 + (1 - core)
            arrived(hs.at[k], hc_recv.at[j, i])
    for c in mine:
        c.wait()
    acc[...] = logits_of(around(1, 2), 0, rows)
    acc[...] += logits_of(around(3, 4), 0, rows)
    ring_step(7, range(PIECES // 2))
    acc[...] += logits_of(around(5, 6), 0, rows)
    ring_step(7, range(PIECES // 2, PIECES))
    acc[...] += logits_of(around(7), 0, rows)

    lanes = 128
    tiles = classes // lanes

    def lane_tiles(v):
        return [v[:, i * lanes:(i + 1) * lanes] for i in range(tiles)]

    def turned_sum(v):
        return jnp.sum(sum(lane_tiles(v)[1:], lane_tiles(v)[0]).T, axis=0, keepdims=True)

    opposite = lax.rem(z + far, groups)
    start_order = [q for pair in zip(right_order[: PIECES // 2], left_order[: PIECES // 2]) for q in pair]
    for q in start_order:
        ring_wait(far - 1, q, halfway(q, True))
        r0 = q * n
        block = pl.ds(r0, n)
        tanh = jnp.tanh((acc[block, :] + logits_of([z, opposite], r0, n)) / softcap)
        student = jnp.exp(softcap * tanh)
        transport = student * student
        stu[block, :] = student
        plan[block, :] = transport
        slope[block, :] = 1.0 - tanh * tanh
        zs0[:, r0:r0 + n] = turned_sum(transport)
        zs0[:, rows + r0:rows + r0 + n] = turned_sum(student)

    z_order = sorted(range(1, groups), key=lambda d: -min(d, groups - d))

    def z_exchange(mine, theirs, i):
        for d in z_order:
            copy(mine, theirs.at[d - 1], zsend.at[i], zrecv.at[i], along(d)).start()

    def z_total(mine, theirs, i):
        copy(theirs, theirs, zsend.at[i], zrecv.at[i], along(1)).wait_recv()
        return mine[...] + jnp.sum(theirs[...], axis=0)

    def c_exchange(mine, theirs, i):
        for n, (dx, dy, dc) in enumerate(OTHERS):
            copy(mine, theirs.at[n], csend.at[i], crecv.at[i], at(dx, dy, dc)).start()

    def c_total(mine, theirs, i):
        copy(theirs, theirs, csend.at[i], crecv.at[i], along(1)).wait_recv()
        return mine[...] + jnp.sum(theirs[...], axis=0)

    def upright(row, r0):
        return jnp.broadcast_to(row[:, r0:r0 + lanes], (lanes, lanes)).T

    z_exchange(zs0, zr0, 0)

    def turn(k, carry):
        t = fs[k].T
        for c in range(2):
            fta[c, lax.rem(k, SIDE), k // SIDE] = t[(2 * c) * quarter:(2 * c + 1) * quarter]
            ftb[c, k // SIDE, lax.rem(k, SIDE)] = t[(2 * c + 1) * quarter:(2 * c + 2) * quarter]
        ht[k] = head_of(k).T
        return carry

    lax.fori_loop(0, groups, turn, 0)
    for r0 in range(0, rows, lanes):
        for c0 in range(0, classes, lanes):
            plan_t[c0:c0 + lanes, r0:r0 + lanes] = plan[r0:r0 + lanes, c0:c0 + lanes].T
    flush(len(sent))

    def early_share(w, r0, count):
        block = pl.ds(r0, count)
        early[w, 0, block, :] = jnp.dot(split[w, block, :], ht[opposite], preferred_element_type=F32).astype(BF)

    def pair_share(w, d):
        both = jnp.concatenate([ht[lax.rem(z + d, groups)], ht[lax.rem(z - d + groups, groups)]], axis=1)
        return jnp.dot(split[w], both, preferred_element_type=F32)

    def early_near(w):
        out = pair_share(w, far - 1).astype(BF)
        early[w, 1] = out[:, :slab]
        early[w, 2] = out[:, slab:]

    def early_send(w, level, q, right):
        i = 0 if right else 1
        src = beyond.at[w, i] if level == 2 else early.at[w, 0 if level == 0 else 1 + i]
        send(part_of(src, q), part_of(early_in.at[w, i, level], q), e_send.at[w, i, level, q],
             e_recv.at[w, i, level, q], along(1 if right else -1))

    def early_wait(w, level, q, right):
        i = 0 if right else 1
        arrived(part_of(early_in.at[w, i, level], q), e_recv.at[w, i, level, q])

    def early_fresh(w):
        for p in range(PIECES // 2):
            early_send(w, 1, left_order[p], True)
            early_send(w, 1, right_order[p], False)

    def early_pass(w):
        for p in range(PIECES // 2):
            for q, right in ((right_order[p], True), (left_order[p], False)):
                i = 0 if right else 1
                early_wait(w, 0, q, right)
                block = pl.ds(q * n, n)
                added = early[w, 1 + i, block, :].astype(F32) + early_in[w, i, 0, block, :].astype(F32)
                early[w, 1 + i, block, :] = added.astype(BF)
                early_send(w, 1, q, right)

    def late_shares(w):
        for m, d in enumerate((far - 2, far - 3)):
            late[w, m] = pair_share(w, d)

    def side(right):
        return slice(0, slab) if right else slice(slab, 2 * slab)

    def early_further(w):
        for p in range(PIECES // 2):
            for q, right in ((left_order[p], True), (right_order[p], False)):
                i = 0 if right else 1
                early_wait(w, 1, q, right)
                block = pl.ds(q * n, n)
                beyond[w, i, block, :] = (late[w, 0, block, side(right)] + early_in[w, i, 1, block, :].astype(F32)).astype(BF)
                early_send(w, 2, q, right)

    def while_columns_travel(it):
        if it == 0:
            for q in start_order:
                block = pl.ds(q * n, n)
                sup = jnp.concatenate([upright(student_inverse, q * n)] * tiles, axis=1)
                split[0, block, :] = (stu[block, :] * sup * slope[block, :]).astype(BF)
                early_share(0, q * n, n)
                early_send(0, 0, q, halfway(q, True))
            early_near(0)
            early_fresh(0)
        elif it == 1:
            early_pass(0)
        elif it == 2:
            late_shares(0)
            early_further(0)

    def while_last_rows_travel(scale):
        for q in start_order:
            block = pl.ds(q * n, n)
            split[1, block, :] = (plan[block, :] * scale * slope[block, :]).astype(BF)
            early_share(1, q * n, n)
            early_send(1, 0, q, halfway(q, True))
        early_near(1)
        early_fresh(1)
        late_shares(1)
        early_pass(1)
        early_further(1)

    ceiling = cap[...].astype(F32).reshape(1, classes) * ratio
    scale = jnp.ones((1, classes), F32)
    both = z_total(zs0, zr0, 0)
    mass = both[:, :rows]
    student_inverse = 1.0 / both[:, rows:]
    for it in range(ITERS):
        inverse = 1.0 / mass
        for c0 in range(0, classes, lanes):
            cs[it, :, c0:c0 + lanes] = turned_sum(plan_t[pl.ds(c0, lanes), :] * inverse)
        c_exchange(cs.at[it], cr.at[it], it)
        while_columns_travel(it)
        total = c_total(cs.at[it], cr.at[it], it)
        scale = jnp.minimum(scale, ceiling / total)
        for r0 in range(0, rows, lanes):
            zs[it, :, r0:r0 + lanes] = turned_sum(plan[pl.ds(r0, lanes), :] * scale)
        z_exchange(zs.at[it], zr.at[it], it + 1)
        if it == ITERS - 1:
            while_last_rows_travel(scale)
        mass = z_total(zs.at[it], zr.at[it], it + 1)

    def rs_send_to(d, q, right):
        i = 0 if right else 1
        src = part.at[d if right or d == far else groups - d]
        dst = from_l if right else from_r
        send(part_of(src, q), part_of(dst.at[d - 1], q), rs_send.at[i, d - 1, q], rs_recv.at[i, d - 1, q],
             along(1 if right else -1))

    def rs_add(d, q, right):
        i = 0 if right else 1
        got = (from_l if right else from_r).at[d]
        mine = part.at[d if right else groups - d]
        arrived(part_of(got, q), rs_recv.at[i, d, q])
        block = pl.ds(q * n, n)
        mine[block, :] = (mine[block, :].astype(F32) + got[block, :].astype(F32)).astype(BF)
        rs_send_to(d, q, right)

    rs_events = [(far - 3, right_order[p], left_order[p]) for p in range(PIECES // 2)]
    rs_events += [(d, left_order[p], right_order[p]) for d in range(far - 4, 0, -1) for p in range(PIECES)]

    def share_pair(d):
        both = jnp.concatenate([ht[lax.rem(z + d, groups)], ht[lax.rem(z - d + groups, groups)]], axis=1)
        out = jnp.dot(grad[...], both, preferred_element_type=F32).astype(BF)
        part[d] = out[:, :slab]
        part[groups - d] = out[:, slab:]

    def share_own():
        part[0] = jnp.dot(grad[...], ht[z], preferred_element_type=F32).astype(BF)

    inverse = 1.0 / mass
    ups = [upright(inverse, q * n) for q in range(PIECES)]

    def merge(q, right, level):
        i = 0 if right else 1
        for w in range(2):
            early_wait(w, level, q, right)
        block = pl.ds(q * n, n)
        student_part, plan_part = (
            late[w, level - 1, block, side(right)] + early_in[w, i, level, block, :].astype(F32) for w in range(2)
        )
        d = far - 1 - level
        part[d if right else groups - d, block, :] = (student_part - ups[q] * plan_part).astype(BF)
        rs_send_to(d, q, right)

    for q in range(PIECES):
        block = pl.ds(q * n, n)
        up = jnp.concatenate([ups[q]] * tiles, axis=1)
        targets = (plan[block, :] * up * scale).astype(BF)
        tgt[block, :] = targets
        sup = jnp.concatenate([upright(student_inverse, q * n)] * tiles, axis=1)
        grad[block, :] = ((stu[block, :] * sup - targets.astype(F32)) * slope[block, :]).astype(BF)

    def next_shares():
        for p in range(PIECES // 2):
            for q, right, k in ((right_order[p], True, far - 3), (left_order[p], False, groups - far + 3)):
                block = pl.ds(q * n, n)
                part[k, block, :] = (late[0, 1, block, side(right)] - ups[q] * late[1, 1, block, side(right)]).astype(BF)

    def summed(*refs):
        out = refs[0].astype(F32)
        for r in refs[1:]:
            out = out + r.astype(F32)
        return out.astype(BF)

    fwd = 1 + 2 * core
    bwd = 3 - 2 * core

    def first_to(half, d):
        return at(d, 0) if half else at(0, d)

    def second_to(half, d):
        return at(0, d) if half else at(d, 0)

    def first_pos(half, d):
        return lax.rem((x if half else y) + d + SIDE, SIDE)

    def second_pos(half, d):
        return lax.rem((y if half else x) + d + SIDE, SIDE)

    def head_share(out, half, c, pair):
        turned = ftb if half else fta
        lhs = jnp.concatenate([turned[c, first_pos(half, i)].reshape(SIDE * quarter, rows) for i in pair], axis=0)
        share = jnp.dot(lhs, grad[...], preferred_element_type=F32).astype(BF)
        for n_, i in enumerate(pair):
            out[half, i] = share[n_ * SIDE * quarter:(n_ + 1) * SIDE * quarter].reshape(SIDE, quarter, classes)

    def give(half, pair):
        head_share(qo, half, 1 - core, pair)
        for i in pair:
            send(qo.at[half, i], core_in.at[half, i], qc_send.at[half, i], qc_recv.at[half, i], at(0, 0, 1))

    def keep(half):
        head_share(qa, half, core, (2, 1))
        head_share(qa, half, core, (3, 0))

    def chip_sum(half):
        for i in (2, 1, 3, 0):
            arrived(core_in.at[half, i], qc_recv.at[half, i])
            qa[half, i] = summed(qa[half, i], core_in[half, i])
            if i == 2:
                send(qa.at[half, 2], first_in.at[half, 0], q1_send.at[half, 0], q1_recv.at[half, 0], first_to(half, way))
            if i == 3:
                send(qa.at[half, bwd], first_in.at[half, 1], q1_send.at[half, 1], q1_recv.at[half, 1],
                     first_to(half, -way))

    def first_mid(half):
        arrived(first_in.at[half, 0], q1_recv.at[half, 0])
        qa[half, fwd] = summed(qa[half, fwd], first_in[half, 0])
        send(qa.at[half, fwd], first_in.at[half, 2], q1_send.at[half, 2], q1_recv.at[half, 2], first_to(half, way))

    def first_end(half):
        arrived(first_in.at[half, 1], q1_recv.at[half, 1])
        arrived(first_in.at[half, 2], q1_recv.at[half, 2])
        qb[half] = summed(qa[half, 0], first_in[half, 1], first_in[half, 2])
        send(qb.at[half, second_pos(half, 2)], second_in.at[half, 0], q2_send.at[half, 0], q2_recv.at[half, 0],
             second_to(half, way))
        send(qb.at[half, second_pos(half, -way)], second_in.at[half, 1], q2_send.at[half, 1], q2_recv.at[half, 1],
             second_to(half, -way))

    def second_mid(half):
        arrived(second_in.at[half, 0], q2_recv.at[half, 0])
        k = second_pos(half, way)
        qb[half, k] = summed(qb[half, k], second_in[half, 0])
        send(qb.at[half, k], second_in.at[half, 2], q2_send.at[half, 2], q2_recv.at[half, 2], second_to(half, way))

    def second_end(half):
        arrived(second_in.at[half, 1], q2_recv.at[half, 1])
        arrived(second_in.at[half, 2], q2_recv.at[half, 2])
        total = summed(qb[half, second_pos(half, 0)], second_in[half, 1], second_in[half, 2])
        ghead[half * quarter:(half + 1) * quarter, :] = total

    give(0, (2, 1))
    give(0, (3, 0))
    for p in range(PIECES // 2):
        merge(right_order[p], True, 1)
        merge(left_order[p], False, 1)
    give(1, (2, 1))
    give(1, (3, 0))
    keep(0)
    for p in range(PIECES // 2):
        merge(left_order[p], True, 2)
        merge(right_order[p], False, 2)
    next_shares()
    keep(1)
    chip_sum(0)
    between = {
        0: [(share_pair, 4)], 1: [(chip_sum, 1)], 3: [(share_pair, 3)], 4: [(share_pair, 2)], 5: [(share_pair, 1)],
        6: [(share_own,)], 7: [(first_mid, 0)], 8: [(first_mid, 1)], 12: [(first_end, 0)], 13: [(first_end, 1)],
        16: [(second_mid, 0)], 17: [(second_mid, 1)],
    }
    old = 0
    for e, (d, to_right, to_left) in enumerate(rs_events):
        if e == 4:
            old = len(sent)
        if e == 12:
            flush(old)
        rs_add(d, to_right, True)
        rs_add(d, to_left, False)
        for task, *what in between.get(e, ()):
            task(*what)

    for p in range(PIECES):
        arrived(part_of(from_l.at[0], left_order[p]), rs_recv.at[0, 0, left_order[p]])
        arrived(part_of(from_r.at[0], right_order[p]), rs_recv.at[1, 0, right_order[p]])
    second_end(0)
    second_end(1)
    gfeat[...] = summed(part[0], from_l[0], from_r[0])

    copy(zr0, zr0, zsend.at[0], zrecv.at[0], along(1)).wait_send()
    for it in range(ITERS):
        copy(zr.at[it], zr.at[it], zsend.at[it + 1], zrecv.at[it + 1], along(1)).wait_send()
        copy(cr.at[it], cr.at[it], csend.at[it], crecv.at[it], along(1)).wait_send()
    flush(len(sent))


def store_kernel(*refs):
    count = len(refs) // 2
    copies = []
    for i in range(count):
        parts = 4 if i == 0 else 1
        rows = refs[i].shape[0] // parts
        for p in range(parts):
            block = pl.ds(p * rows, rows)
            copies.append(pltpu.make_async_copy(refs[i].at[block], refs[count + i].at[block], refs[-1].at[len(copies)]))
    for c in copies:
        c.start()
    for c in copies:
        c.wait()


def store(results):
    return pl.pallas_call(
        store_kernel,
        out_shape=tuple(jax.ShapeDtypeStruct(r.shape, r.dtype) for r in results),
        in_specs=[pl.BlockSpec(memory_space=pltpu.VMEM)] * len(results),
        out_specs=(pl.BlockSpec(memory_space=pltpu.HBM),) * len(results),
        scratch_shapes=[pltpu.SemaphoreType.DMA((len(results) + 3,))],
        compiler_params=pltpu.CompilerParams(vmem_limit_bytes=4 << 20),
    )(*results)


def solution(mesh):
    groups = mesh.shape["cls"]
    samples = mesh.shape["sample"]

    def per_device(features, head, class_cap):
        rows, slab = features.shape
        depth, classes = head.shape
        width = slab * groups
        chips = samples // 2
        far = groups // 2
        ratio = rows * samples / (classes * groups)
        V = pltpu.VMEM
        dma = pltpu.SemaphoreType.DMA
        scratch = [
            V((groups, rows, slab), BF), V((samples, depth, classes), BF),
            V((2, SIDE, SIDE, depth // 2, rows), BF), V((2, SIDE, SIDE, depth // 2, rows), BF), V((groups, classes, slab), BF),
            V((rows, classes), F32), V((rows, classes), F32), V((rows, classes), F32), V((classes, rows), F32),
            V((rows, classes), F32),
            V((rows, classes), BF),
            V((groups, rows, slab), BF), V((far, rows, slab), BF), V((far, rows, slab), BF),
            V((2, rows, classes), BF), V((2, 3, rows, slab), BF), V((2, 2, 3, rows, slab), BF), V((2, 2, rows, 2 * slab), F32),
            V((2, 2, rows, slab), BF),
            V((2, SIDE, SIDE, depth // 2, classes), BF), V((2, SIDE, SIDE, depth // 2, classes), BF),
            V((2, SIDE, SIDE, depth // 2, classes), BF), V((2, 3, SIDE, depth // 2, classes), BF),
            V((2, SIDE, depth // 2, classes), BF), V((2, 3, depth // 2, classes), BF),
            V((1, 2 * rows), F32), V((ITERS, 1, rows), F32),
            V((groups - 1, 1, 2 * rows), F32), V((ITERS, groups - 1, 1, rows), F32),
            V((ITERS, 1, classes), F32), V((ITERS, samples - 1, 1, classes), F32),
            dma((2, far, PIECES)), dma((2, far, PIECES)), dma((3,)), dma((3,)), dma((4, 3)), dma((4, 3)), dma((4, 4)), dma((4, 4)),
            dma((ITERS + 1,)), dma((ITERS + 1,)), dma((ITERS,)), dma((ITERS,)),
            V((classes,), BF), dma((3,)), dma((2, 2, 3, PIECES)), dma((2, 2, 3, PIECES)),
            dma((2, far, PIECES)), dma((2, far, PIECES)), dma((2, 4)), dma((2, 4)), dma((2, 3)), dma((2, 3)), dma((2, 3)), dma((2, 3)),
        ]
        vmem = pl.BlockSpec(memory_space=pltpu.VMEM)
        hbm = pl.BlockSpec(memory_space=pltpu.HBM)
        results = pl.pallas_call(
            functools.partial(kernel, rows, width, classes, groups, ratio),
            out_shape=(
                jax.ShapeDtypeStruct((rows, classes), BF),
                jax.ShapeDtypeStruct((rows, slab), BF),
                jax.ShapeDtypeStruct((depth, classes), BF),
            ),
            in_specs=[hbm] * 3,
            out_specs=(vmem,) * 3,
            scratch_shapes=scratch,
            compiler_params=pltpu.CompilerParams(
                collective_id=0, has_side_effects=True, vmem_limit_bytes=48 << 20
            ),
        )(*(pltpu.with_memory_space_constraint(a, pltpu.HBM) for a in (features, head, class_cap)))
        return store(results)

    return jax.shard_map(
        per_device,
        mesh=mesh,
        in_specs=(P("sample", "cls"), P("sample", "cls"), P("cls")),
        out_specs=(P("sample", "cls"), P("sample", "cls"), P("sample", "cls")),
        check_vma=False,
    )
```

```python
import functools
import jax
import jax.numpy as jnp
from jax import lax
from jax.experimental import pallas as pl
from jax.experimental.pallas import tpu as pltpu
from jax.sharding import PartitionSpec as P

ITERS = 3
softcap = 15.0
sharpen = 2.0
MESH = pl.DeviceIdType.MESH
SIDE = 4
PIECES = 4
BF = jnp.bfloat16
F32 = jnp.float32

OTHERS = sorted(
    ((dx, dy, dc) for dx in range(SIDE) for dy in range(SIDE) for dc in range(2) if dx or dy or dc),
    key=lambda o: -(min(o[0], SIDE - o[0]) + min(o[1], SIDE - o[1]) + 0.5 * o[2]),
)


def kernel(
    rows, width, classes, groups, ratio,
    feat, head, cap_in,
    tgt, gfeat, ghead,
    fs, hs, fta, ftb, ht, acc, stu, plan, plan_t, slope, grad,
    part, from_l, from_r,
    split, early, early_in, late, beyond,
    qo, core_in, qa, first_in, qb, second_in,
    zs0, zs, zr0, zr, cs, cr,
    ag_send, ag_recv, h_send, hx_recv, hy_recv, hc_recv,
    zsend, zrecv, csend, crecv, cap, local, e_send, e_recv,
    rs_send, rs_recv, qc_send, qc_recv, q1_send, q1_recv, q2_send, q2_recv,
):
    s = lax.axis_index("sample")
    z = lax.axis_index("cls")
    core = lax.rem(s, 2)
    chip = s // 2
    y = lax.rem(chip, SIDE)
    x = chip // SIDE
    way = 1 - 2 * core
    n = rows // PIECES
    slab = width // groups
    far = groups // 2
    quarter = slab // 4

    def at(dx, dy, flip=0):
        c = lax.rem(core + flip, 2)
        return ((lax.rem(x + dx + SIDE, SIDE) * SIDE + lax.rem(y + dy + SIDE, SIDE)) * 2 + c, z)

    def along(d):
        return (s, lax.rem(z + d + groups, groups))

    def slot(dx, dy):
        return (lax.rem(x + dx + SIDE, SIDE) * SIDE + lax.rem(y + dy + SIDE, SIDE)) * 2 + core

    def copy(src, dst, ssem, rsem, to):
        return pltpu.make_async_remote_copy(
            src_ref=src, dst_ref=dst, send_sem=ssem, recv_sem=rsem, device_id=to, device_id_type=MESH
        )

    def send(src, dst, ssem, rsem, to):
        copy(src, dst, ssem, rsem, to).start()

    def left(ref, ssem):
        copy(ref, ref, ssem, ssem, along(1)).wait_send()

    def arrived(ref, rsem):
        copy(ref, ref, rsem, rsem, along(1)).wait_recv()

    barrier = pltpu.get_barrier_semaphore()
    near = [along(1), along(-1), at(1, 0), at(-1, 0), at(0, 1), at(0, -1), at(0, 0, 1)]
    for to in near:
        pl.semaphore_signal(barrier, inc=1, device_id=to, device_id_type=MESH)
    pl.semaphore_wait(barrier, len(near))

    def part_of(ref, q):
        return ref.at[pl.ds(q * n, n)]

    right_order = tuple(range(PIECES))
    left_order = right_order[PIECES // 2:] + right_order[:PIECES // 2]

    def halfway(q, forward):
        return (q < PIECES // 2) == forward

    def ring_send(t, q, forward):
        hop = 1 if forward else -1
        k = lax.rem(z - hop * t + groups, groups)
        src = part_of(feat, q) if t == 0 else part_of(fs.at[k], q)
        i = 0 if forward else 1
        send(src, part_of(fs.at[k], q), ag_send.at[0], ag_recv.at[i, t, q], along(hop))

    def ring_wait(t, q, forward):
        hop = 1 if forward else -1
        k = lax.rem(z - hop * (t + 1) + groups, groups)
        arrived(part_of(fs.at[k], q), ag_recv.at[0 if forward else 1, t, q])

    def ring_step(t, pieces=range(PIECES)):
        for p in pieces:
            for forward, q in ((True, right_order[p]), (False, left_order[p])):
                ring_wait(t - 1, q, forward)
                if t < far - 1 or halfway(q, forward):
                    ring_send(t, q, forward)

    x_off = (0, -1, 1, 2)
    own = 2 * chip + core

    def to_y(j, src):
        k = slot(x_off[j], 0)
        send(src, hs.at[k], h_send.at[0], hy_recv.at[j, 0], at(0, 1))
        send(src, hs.at[k], h_send.at[0], hy_recv.at[j, 1], at(0, -1))

    def to_core(j, i, src):
        k = slot(x_off[j], x_off[i])
        send(src, hs.at[k], h_send.at[0], hc_recv.at[0], at(0, 0, 1))

    for p in range(PIECES):
        ring_send(0, right_order[p], True)
        ring_send(0, left_order[p], False)
    send(head, hs.at[own], h_send.at[0], hx_recv.at[0], at(1, 0))
    send(head, hs.at[own], h_send.at[0], hx_recv.at[1], at(-1, 0))
    to_y(0, head)
    to_core(0, 0, head)
    mine = [
        pltpu.make_async_copy(feat, fs.at[z], local.at[0]),
        pltpu.make_async_copy(head, hs.at[own], local.at[1]),
        pltpu.make_async_copy(cap_in, cap, local.at[2]),
    ]
    for c in mine:
        c.start()

    def x_near():
        behind = slot(-way, 0)
        arrived(hs.at[behind], hx_recv.at[core])
        send(hs.at[behind], hs.at[behind], h_send.at[0], hx_recv.at[2], at(way, 0))
        arrived(hs.at[slot(way, 0)], hx_recv.at[1 - core])
        for j in (1, 2):
            to_y(j, hs.at[slot(x_off[j], 0)])
            to_core(j, 0, hs.at[slot(x_off[j], 0)])

    def x_far():
        arrived(hs.at[slot(2, 0)], hx_recv.at[2])
        to_y(3, hs.at[slot(2, 0)])
        to_core(3, 0, hs.at[slot(2, 0)])

    def y_pair(j):
        k = slot(x_off[j], -way)
        arrived(hs.at[k], hy_recv.at[j, core])
        send(hs.at[k], hs.at[k], h_send.at[0], hy_recv.at[j, 2], at(0, way))
        arrived(hs.at[slot(x_off[j], way)], hy_recv.at[j, 1 - core])
        to_core(j, 1, hs.at[slot(x_off[j], -1)])
        to_core(j, 2, hs.at[slot(x_off[j], 1)])

    def y_far(j):
        k = slot(x_off[j], 2)
        arrived(hs.at[k], hy_recv.at[j, 2])
        to_core(j, 3, hs.at[k])

    x_near()
    ring_step(1)
    y_pair(0)
    ring_step(2, range(PIECES // 2))
    x_far()
    ring_step(2, range(PIECES // 2, PIECES))
    y_far(0)
    y_pair(1)
    ring_step(3, range(PIECES // 2))
    y_pair(2)
    ring_step(3, range(PIECES // 2, PIECES))
    y_far(1)
    y_pair(3)
    ring_step(4, range(PIECES // 2))
    y_far(2)
    ring_step(4, range(PIECES // 2, PIECES))
    y_far(3)
    ring_step(5)

    def head_of(k):
        return hs[pl.ds(2 * k, 2)].reshape(slab, classes)

    def logits_of(slots, r0, count):
        left = jnp.concatenate([fs[k, pl.ds(r0, count), :] for k in slots], axis=1)
        right = jnp.concatenate([head_of(k) for k in slots], axis=0)
        return jnp.dot(left, right, preferred_element_type=F32)

    def around(*distances):
        return [lax.rem(z + d, groups) for e in distances for d in (groups - e, e)]

    ring_step(6)
    arrived(hs.at[pl.ds(0, 4 * SIDE)], hc_recv.at[0])
    for c in mine:
        c.wait()
    acc[...] = logits_of(around(1, 2), 0, rows)
    acc[...] += logits_of(around(3, 4), 0, rows)
    ring_step(7, range(PIECES // 2))
    acc[...] += logits_of(around(5, 6), 0, rows)
    ring_step(7, range(PIECES // 2, PIECES))
    acc[...] += logits_of(around(7), 0, rows)

    lanes = 128
    tiles = classes // lanes

    def lane_tiles(v):
        return [v[:, i * lanes:(i + 1) * lanes] for i in range(tiles)]

    def turned_sum(v):
        return jnp.sum(sum(lane_tiles(v)[1:], lane_tiles(v)[0]).T, axis=0, keepdims=True)

    opposite = lax.rem(z + far, groups)
    start_order = [q for pair in zip(right_order[: PIECES // 2], left_order[: PIECES // 2]) for q in pair]
    for q in start_order:
        ring_wait(far - 1, q, halfway(q, True))
        r0 = q * n
        block = pl.ds(r0, n)
        tanh = jnp.tanh((acc[block, :] + logits_of([z, opposite], r0, n)) / softcap)
        student = jnp.exp(softcap * tanh)
        transport = student * student
        stu[block, :] = student
        plan[block, :] = transport
        slope[block, :] = 1.0 - tanh * tanh
        zs0[:, r0:r0 + n] = turned_sum(transport)
        zs0[:, rows + r0:rows + r0 + n] = turned_sum(student)

    z_order = sorted(range(1, groups), key=lambda d: -min(d, groups - d))

    def z_exchange(mine, theirs, i):
        for d in z_order:
            copy(mine, theirs.at[d - 1], zsend.at[i], zrecv.at[i], along(d)).start()

    def z_total(mine, theirs, i):
        copy(theirs, theirs, zsend.at[i], zrecv.at[i], along(1)).wait_recv()
        return mine[...] + jnp.sum(theirs[...], axis=0)

    def c_exchange(mine, theirs, i):
        for n, (dx, dy, dc) in enumerate(OTHERS):
            copy(mine, theirs.at[n], csend.at[i], crecv.at[i], at(dx, dy, dc)).start()

    def c_total(mine, theirs, i):
        copy(theirs, theirs, csend.at[i], crecv.at[i], along(1)).wait_recv()
        return mine[...] + jnp.sum(theirs[...], axis=0)

    def upright(row, r0):
        return jnp.broadcast_to(row[:, r0:r0 + lanes], (lanes, lanes)).T

    z_exchange(zs0, zr0, 0)

    def turn(k, carry):
        t = fs[k].T
        for c in range(2):
            fta[c, lax.rem(k, SIDE), k // SIDE] = t[(2 * c) * quarter:(2 * c + 1) * quarter]
            ftb[c, k // SIDE, lax.rem(k, SIDE)] = t[(2 * c + 1) * quarter:(2 * c + 2) * quarter]
        ht[k] = head_of(k).T
        return carry

    lax.fori_loop(0, groups, turn, 0)
    for r0 in range(0, rows, lanes):
        for c0 in range(0, classes, lanes):
            plan_t[c0:c0 + lanes, r0:r0 + lanes] = plan[r0:r0 + lanes, c0:c0 + lanes].T
    left(fs.at[pl.ds(0, groups - 1)], ag_send.at[0])
    left(hs.at[pl.ds(0, hs.shape[0] - 1)], h_send.at[0])

    def early_share(w, r0, count):
        block = pl.ds(r0, count)
        early[w, 0, block, :] = jnp.dot(split[w, block, :], ht[opposite], preferred_element_type=F32).astype(BF)

    def pair_share(w, d):
        both = jnp.concatenate([ht[lax.rem(z + d, groups)], ht[lax.rem(z - d + groups, groups)]], axis=1)
        return jnp.dot(split[w], both, preferred_element_type=F32)

    def early_near(w):
        out = pair_share(w, far - 1).astype(BF)
        early[w, 1] = out[:, :slab]
        early[w, 2] = out[:, slab:]

    def early_send(w, level, q, right):
        i = 0 if right else 1
        src = beyond.at[w, i] if level == 2 else early.at[w, 0 if level == 0 else 1 + i]
        send(part_of(src, q), part_of(early_in.at[w, i, level], q), e_send.at[w],
             e_recv.at[w, i, level % 2, q], along(1 if right else -1))

    def early_wait(w, level, q, right):
        i = 0 if right else 1
        arrived(part_of(early_in.at[w, i, level], q), e_recv.at[w, i, level % 2, q])

    def early_fresh(w):
        for p in range(PIECES // 2):
            early_send(w, 1, left_order[p], True)
            early_send(w, 1, right_order[p], False)

    def early_pass(w):
        for p in range(PIECES // 2):
            for q, right in ((right_order[p], True), (left_order[p], False)):
                i = 0 if right else 1
                early_wait(w, 0, q, right)
                block = pl.ds(q * n, n)
                added = early[w, 1 + i, block, :].astype(F32) + early_in[w, i, 0, block, :].astype(F32)
                early[w, 1 + i, block, :] = added.astype(BF)
                early_send(w, 1, q, right)

    def late_shares(w):
        for m, d in enumerate((far - 2, far - 3)):
            late[w, m] = pair_share(w, d)

    def side(right):
        return slice(0, slab) if right else slice(slab, 2 * slab)

    def early_further(w):
        for p in range(PIECES // 2):
            for q, right in ((left_order[p], True), (right_order[p], False)):
                i = 0 if right else 1
                early_wait(w, 1, q, right)
                block = pl.ds(q * n, n)
                beyond[w, i, block, :] = (late[w, 0, block, side(right)] + early_in[w, i, 1, block, :].astype(F32)).astype(BF)
                early_send(w, 2, q, right)

    def while_columns_travel(it):
        if it == 0:
            for q in start_order:
                block = pl.ds(q * n, n)
                sup = jnp.concatenate([upright(student_inverse, q * n)] * tiles, axis=1)
                split[0, block, :] = (stu[block, :] * sup * slope[block, :]).astype(BF)
                early_share(0, q * n, n)
                early_send(0, 0, q, halfway(q, True))
            early_near(0)
            early_fresh(0)
        elif it == 1:
            early_pass(0)
        elif it == 2:
            late_shares(0)
            early_further(0)

    def while_last_rows_travel(scale):
        for q in start_order:
            block = pl.ds(q * n, n)
            split[1, block, :] = (plan[block, :] * scale * slope[block, :]).astype(BF)
            early_share(1, q * n, n)
            early_send(1, 0, q, halfway(q, True))
        early_near(1)
        early_fresh(1)
        late_shares(1)
        early_pass(1)
        early_further(1)

    ceiling = cap[...].astype(F32).reshape(1, classes) * ratio
    scale = jnp.ones((1, classes), F32)
    both = z_total(zs0, zr0, 0)
    mass = both[:, :rows]
    student_inverse = 1.0 / both[:, rows:]
    for it in range(ITERS):
        inverse = 1.0 / mass
        for c0 in range(0, classes, lanes):
            cs[it, :, c0:c0 + lanes] = turned_sum(plan_t[pl.ds(c0, lanes), :] * inverse)
        c_exchange(cs.at[it], cr.at[it], it)
        while_columns_travel(it)
        total = c_total(cs.at[it], cr.at[it], it)
        scale = jnp.minimum(scale, ceiling / total)
        for r0 in range(0, rows, lanes):
            zs[it, :, r0:r0 + lanes] = turned_sum(plan[pl.ds(r0, lanes), :] * scale)
        z_exchange(zs.at[it], zr.at[it], it + 1)
        if it == ITERS - 1:
            while_last_rows_travel(scale)
        mass = z_total(zs.at[it], zr.at[it], it + 1)

    def rs_send_to(d, q, right):
        i = 0 if right else 1
        src = part.at[d if right or d == far else groups - d]
        dst = from_l if right else from_r
        send(part_of(src, q), part_of(dst.at[d - 1], q), rs_send.at[0], rs_recv.at[i, d - 1, q],
             along(1 if right else -1))

    def rs_add(d, q, right):
        i = 0 if right else 1
        got = (from_l if right else from_r).at[d]
        mine = part.at[d if right else groups - d]
        arrived(part_of(got, q), rs_recv.at[i, d, q])
        block = pl.ds(q * n, n)
        mine[block, :] = (mine[block, :].astype(F32) + got[block, :].astype(F32)).astype(BF)
        rs_send_to(d, q, right)

    rs_events = [(far - 3, right_order[p], left_order[p]) for p in range(PIECES // 2)]
    rs_events += [(d, left_order[p], right_order[p]) for d in range(far - 4, 0, -1) for p in range(PIECES)]

    def share_pair(d):
        both = jnp.concatenate([ht[lax.rem(z + d, groups)], ht[lax.rem(z - d + groups, groups)]], axis=1)
        out = jnp.dot(grad[...], both, preferred_element_type=F32).astype(BF)
        part[d] = out[:, :slab]
        part[groups - d] = out[:, slab:]

    def share_own():
        part[0] = jnp.dot(grad[...], ht[z], preferred_element_type=F32).astype(BF)

    inverse = 1.0 / mass
    ups = [upright(inverse, q * n) for q in range(PIECES)]

    def merge(q, right, level):
        i = 0 if right else 1
        for w in range(2):
            early_wait(w, level, q, right)
        block = pl.ds(q * n, n)
        student_part, plan_part = (
            late[w, level - 1, block, side(right)] + early_in[w, i, level, block, :].astype(F32) for w in range(2)
        )
        d = far - 1 - level
        part[d if right else groups - d, block, :] = (student_part - ups[q] * plan_part).astype(BF)
        rs_send_to(d, q, right)

    for q in range(PIECES):
        block = pl.ds(q * n, n)
        up = jnp.concatenate([ups[q]] * tiles, axis=1)
        targets = (plan[block, :] * up * scale).astype(BF)
        tgt[block, :] = targets
        sup = jnp.concatenate([upright(student_inverse, q * n)] * tiles, axis=1)
        grad[block, :] = ((stu[block, :] * sup - targets.astype(F32)) * slope[block, :]).astype(BF)

    def next_shares():
        for p in range(PIECES // 2):
            for q, right, k in ((right_order[p], True, far - 3), (left_order[p], False, groups - far + 3)):
                block = pl.ds(q * n, n)
                part[k, block, :] = (late[0, 1, block, side(right)] - ups[q] * late[1, 1, block, side(right)]).astype(BF)

    def summed(*refs):
        out = refs[0].astype(F32)
        for r in refs[1:]:
            out = out + r.astype(F32)
        return out.astype(BF)

    fwd = 1 + 2 * core
    bwd = 3 - 2 * core

    def first_to(half, d):
        return at(d, 0) if half else at(0, d)

    def second_to(half, d):
        return at(0, d) if half else at(d, 0)

    def first_pos(half, d):
        return lax.rem((x if half else y) + d + SIDE, SIDE)

    def second_pos(half, d):
        return lax.rem((y if half else x) + d + SIDE, SIDE)

    def head_share(out, half, c, pair):
        turned = ftb if half else fta
        lhs = jnp.concatenate([turned[c, first_pos(half, i)].reshape(SIDE * quarter, rows) for i in pair], axis=0)
        share = jnp.dot(lhs, grad[...], preferred_element_type=F32).astype(BF)
        for n_, i in enumerate(pair):
            out[half, i] = share[n_ * SIDE * quarter:(n_ + 1) * SIDE * quarter].reshape(SIDE, quarter, classes)

    def give(half, pair):
        head_share(qo, half, 1 - core, pair)
        for i in pair:
            send(qo.at[half, i], core_in.at[half, i], qc_send.at[0], qc_recv.at[half, i], at(0, 0, 1))

    def keep(half):
        head_share(qa, half, core, (2, 1))
        head_share(qa, half, core, (3, 0))

    def chip_sum(half):
        for i in (2, 1, 3, 0):
            arrived(core_in.at[half, i], qc_recv.at[half, i])
            qa[half, i] = summed(qa[half, i], core_in[half, i])
            if i == 2:
                send(qa.at[half, 2], first_in.at[half, 0], q1_send.at[0], q1_recv.at[half, 0], first_to(half, way))
            if i == 3:
                send(qa.at[half, bwd], first_in.at[half, 1], q1_send.at[0], q1_recv.at[half, 1],
                     first_to(half, -way))

    def first_mid(half):
        arrived(first_in.at[half, 0], q1_recv.at[half, 0])
        qa[half, fwd] = summed(qa[half, fwd], first_in[half, 0])
        send(qa.at[half, fwd], first_in.at[half, 2], q1_send.at[0], q1_recv.at[half, 2], first_to(half, way))

    def first_end(half):
        arrived(first_in.at[half, 1], q1_recv.at[half, 1])
        arrived(first_in.at[half, 2], q1_recv.at[half, 2])
        qb[half] = summed(qa[half, 0], first_in[half, 1], first_in[half, 2])
        send(qb.at[half, second_pos(half, 2)], second_in.at[half, 0], q2_send.at[0], q2_recv.at[half, 0],
             second_to(half, way))
        send(qb.at[half, second_pos(half, -way)], second_in.at[half, 1], q2_send.at[0], q2_recv.at[half, 1],
             second_to(half, -way))

    def second_mid(half):
        arrived(second_in.at[half, 0], q2_recv.at[half, 0])
        k = second_pos(half, way)
        qb[half, k] = summed(qb[half, k], second_in[half, 0])
        send(qb.at[half, k], second_in.at[half, 2], q2_send.at[0], q2_recv.at[half, 2], second_to(half, way))

    def second_end(half):
        arrived(second_in.at[half, 1], q2_recv.at[half, 1])
        arrived(second_in.at[half, 2], q2_recv.at[half, 2])
        total = summed(qb[half, second_pos(half, 0)], second_in[half, 1], second_in[half, 2])
        ghead[half * quarter:(half + 1) * quarter, :] = total

    give(0, (2, 1))
    give(0, (3, 0))
    for p in range(PIECES // 2):
        merge(right_order[p], True, 1)
        merge(left_order[p], False, 1)
    give(1, (2, 1))
    give(1, (3, 0))
    keep(0)
    for p in range(PIECES // 2):
        merge(left_order[p], True, 2)
        merge(right_order[p], False, 2)
    next_shares()
    keep(1)
    chip_sum(0)
    between = {
        0: [(share_pair, 4)], 1: [(chip_sum, 1)], 3: [(share_pair, 3)], 4: [(share_pair, 2)], 5: [(share_pair, 1)],
        6: [(share_own,)], 7: [(first_mid, 0)], 8: [(first_mid, 1)], 12: [(first_end, 0)], 13: [(first_end, 1)],
        16: [(second_mid, 0)], 17: [(second_mid, 1)],
    }
    for e, (d, to_right, to_left) in enumerate(rs_events):
        if e == 12:
            for w in range(2):
                left(part.at[pl.ds(0, 4)], e_send.at[w])
            left(qo, qc_send.at[0])
        rs_add(d, to_right, True)
        rs_add(d, to_left, False)
        for task, *what in between.get(e, ()):
            task(*what)

    for p in range(PIECES):
        arrived(part_of(from_l.at[0], left_order[p]), rs_recv.at[0, 0, left_order[p]])
        arrived(part_of(from_r.at[0], right_order[p]), rs_recv.at[1, 0, right_order[p]])
    second_end(0)
    second_end(1)
    gfeat[...] = summed(part[0], from_l[0], from_r[0])

    copy(zr0, zr0, zsend.at[0], zrecv.at[0], along(1)).wait_send()
    for it in range(ITERS):
        copy(zr.at[it], zr.at[it], zsend.at[it + 1], zrecv.at[it + 1], along(1)).wait_send()
        copy(cr.at[it], cr.at[it], csend.at[it], crecv.at[it], along(1)).wait_send()
    left(part.at[pl.ds(0, far + 3)], rs_send.at[0])
    left(first_in, q1_send.at[0])
    left(second_in, q2_send.at[0])


def store_kernel(*refs):
    count = len(refs) // 2
    copies = []
    for i in range(count):
        parts = 4 if i == 0 else 1
        rows = refs[i].shape[0] // parts
        for p in range(parts):
            block = pl.ds(p * rows, rows)
            copies.append(pltpu.make_async_copy(refs[i].at[block], refs[count + i].at[block], refs[-1].at[len(copies)]))
    for c in copies:
        c.start()
    for c in copies:
        c.wait()


def store(results):
    return pl.pallas_call(
        store_kernel,
        out_shape=tuple(jax.ShapeDtypeStruct(r.shape, r.dtype) for r in results),
        in_specs=[pl.BlockSpec(memory_space=pltpu.VMEM)] * len(results),
        out_specs=(pl.BlockSpec(memory_space=pltpu.HBM),) * len(results),
        scratch_shapes=[pltpu.SemaphoreType.DMA((len(results) + 3,))],
        compiler_params=pltpu.CompilerParams(vmem_limit_bytes=4 << 20),
    )(*results)


def solution(mesh):
    groups = mesh.shape["cls"]
    samples = mesh.shape["sample"]

    def per_device(features, head, class_cap):
        rows, slab = features.shape
        depth, classes = head.shape
        width = slab * groups
        chips = samples // 2
        far = groups // 2
        ratio = rows * samples / (classes * groups)
        V = pltpu.VMEM
        dma = pltpu.SemaphoreType.DMA
        scratch = [
            V((groups, rows, slab), BF), V((samples, depth, classes), BF),
            V((2, SIDE, SIDE, depth // 2, rows), BF), V((2, SIDE, SIDE, depth // 2, rows), BF), V((groups, classes, slab), BF),
            V((rows, classes), F32), V((rows, classes), F32), V((rows, classes), F32), V((classes, rows), F32),
            V((rows, classes), F32),
            V((rows, classes), BF),
            V((groups, rows, slab), BF), V((far, rows, slab), BF), V((far, rows, slab), BF),
            V((2, rows, classes), BF), V((2, 3, rows, slab), BF), V((2, 2, 3, rows, slab), BF), V((2, 2, rows, 2 * slab), F32),
            V((2, 2, rows, slab), BF),
            V((2, SIDE, SIDE, depth // 2, classes), BF), V((2, SIDE, SIDE, depth // 2, classes), BF),
            V((2, SIDE, SIDE, depth // 2, classes), BF), V((2, 3, SIDE, depth // 2, classes), BF),
            V((2, SIDE, depth // 2, classes), BF), V((2, 3, depth // 2, classes), BF),
            V((1, 2 * rows), F32), V((ITERS, 1, rows), F32),
            V((groups - 1, 1, 2 * rows), F32), V((ITERS, groups - 1, 1, rows), F32),
            V((ITERS, 1, classes), F32), V((ITERS, samples - 1, 1, classes), F32),
            dma((1,)), dma((2, far, PIECES)), dma((1,)), dma((3,)), dma((4, 3)), dma((1,)),
            dma((ITERS + 1,)), dma((ITERS + 1,)), dma((ITERS,)), dma((ITERS,)),
            V((classes,), BF), dma((3,)), dma((2,)), dma((2, 2, 2, PIECES)),
            dma((1,)), dma((2, far - 2, PIECES)), dma((1,)), dma((2, 4)), dma((1,)), dma((2, 3)), dma((1,)), dma((2, 3)),
        ]
        vmem = pl.BlockSpec(memory_space=pltpu.VMEM)
        hbm = pl.BlockSpec(memory_space=pltpu.HBM)
        results = pl.pallas_call(
            functools.partial(kernel, rows, width, classes, groups, ratio),
            out_shape=(
                jax.ShapeDtypeStruct((rows, classes), BF),
                jax.ShapeDtypeStruct((rows, slab), BF),
                jax.ShapeDtypeStruct((depth, classes), BF),
            ),
            in_specs=[hbm] * 3,
            out_specs=(vmem,) * 3,
            scratch_shapes=scratch,
            compiler_params=pltpu.CompilerParams(
                collective_id=0, has_side_effects=True, vmem_limit_bytes=48 << 20
            ),
        )(*(pltpu.with_memory_space_constraint(a, pltpu.HBM) for a in (features, head, class_cap)))
        return store(results)

    return jax.shard_map(
        per_device,
        mesh=mesh,
        in_specs=(P("sample", "cls"), P("sample", "cls"), P("cls")),
        out_specs=(P("sample", "cls"), P("sample", "cls"), P("sample", "cls")),
        check_vma=False,
    )
```

```python
import functools
import jax
import jax.numpy as jnp
from jax import lax
from jax.experimental import pallas as pl
from jax.experimental.pallas import tpu as pltpu
from jax.sharding import PartitionSpec as P

ITERS = 3
softcap = 15.0
sharpen = 2.0
MESH = pl.DeviceIdType.MESH
SIDE = 4
PIECES = 4
BF = jnp.bfloat16
F32 = jnp.float32

OTHERS = sorted(
    ((dx, dy, dc) for dx in range(SIDE) for dy in range(SIDE) for dc in range(2) if dx or dy or dc),
    key=lambda o: -(min(o[0], SIDE - o[0]) + min(o[1], SIDE - o[1]) + 0.5 * o[2]),
)


def kernel(
    rows, width, classes, groups, ratio,
    feat, head, cap_in,
    tgt, gfeat, ghead,
    fs, hs, fta, ftb, ht, acc, stu, plan, plan_t, slope, grad,
    part, from_l, from_r,
    split, early, early_in, late, beyond,
    qo, core_in, qa, first_in, qb, second_in,
    zs0, zs, zr0, zr, cs, cr,
    ag_send, ring_recv, h_send, hx_recv, hy_recv, hc_recv,
    zsend, zrecv, csend, crecv, cap, local, e_send,
    rs_send, qc_send, qc_recv, q1_send, q1_recv, q2_send, q2_recv,
):
    s = lax.axis_index("sample")
    z = lax.axis_index("cls")
    core = lax.rem(s, 2)
    chip = s // 2
    y = lax.rem(chip, SIDE)
    x = chip // SIDE
    way = 1 - 2 * core
    n = rows // PIECES
    slab = width // groups
    far = groups // 2
    quarter = slab // 4

    def at(dx, dy, flip=0):
        c = lax.rem(core + flip, 2)
        return ((lax.rem(x + dx + SIDE, SIDE) * SIDE + lax.rem(y + dy + SIDE, SIDE)) * 2 + c, z)

    def along(d):
        return (s, lax.rem(z + d + groups, groups))

    def slot(dx, dy):
        return (lax.rem(x + dx + SIDE, SIDE) * SIDE + lax.rem(y + dy + SIDE, SIDE)) * 2 + core

    def copy(src, dst, ssem, rsem, to):
        return pltpu.make_async_remote_copy(
            src_ref=src, dst_ref=dst, send_sem=ssem, recv_sem=rsem, device_id=to, device_id_type=MESH
        )

    def send(src, dst, ssem, rsem, to):
        copy(src, dst, ssem, rsem, to).start()

    def left(ref, ssem):
        copy(ref, ref, ssem, ssem, along(1)).wait_send()

    def arrived(ref, rsem):
        copy(ref, ref, rsem, rsem, along(1)).wait_recv()

    barrier = pltpu.get_barrier_semaphore()
    near = [along(1), along(-1), at(1, 0), at(-1, 0), at(0, 1), at(0, -1), at(0, 0, 1)]
    for to in near:
        pl.semaphore_signal(barrier, inc=1, device_id=to, device_id_type=MESH)
    pl.semaphore_wait(barrier, len(near))

    def part_of(ref, q):
        return ref.at[pl.ds(q * n, n)]

    right_order = tuple(range(PIECES))
    left_order = right_order[PIECES // 2:] + right_order[:PIECES // 2]

    def halfway(q, forward):
        return (q < PIECES // 2) == forward

    def ring_send(t, q, forward):
        hop = 1 if forward else -1
        k = lax.rem(z - hop * t + groups, groups)
        src = part_of(feat, q) if t == 0 else part_of(fs.at[k], q)
        i = 0 if forward else 1
        send(src, part_of(fs.at[k], q), ag_send.at[0], ring_recv.at[i, t, q], along(hop))

    def ring_wait(t, q, forward):
        hop = 1 if forward else -1
        k = lax.rem(z - hop * (t + 1) + groups, groups)
        arrived(part_of(fs.at[k], q), ring_recv.at[0 if forward else 1, t, q])

    def ring_step(t, pieces=range(PIECES)):
        for p in pieces:
            for forward, q in ((True, right_order[p]), (False, left_order[p])):
                ring_wait(t - 1, q, forward)
                if t < far - 1 or halfway(q, forward):
                    ring_send(t, q, forward)

    x_off = (0, -1, 1, 2)
    own = 2 * chip + core

    def to_y(j, src):
        k = slot(x_off[j], 0)
        send(src, hs.at[k], h_send.at[0], hy_recv.at[j, 0], at(0, 1))
        send(src, hs.at[k], h_send.at[0], hy_recv.at[j, 1], at(0, -1))

    def to_core(j, i, src):
        k = slot(x_off[j], x_off[i])
        send(src, hs.at[k], h_send.at[0], hc_recv.at[0], at(0, 0, 1))

    for p in range(PIECES):
        ring_send(0, right_order[p], True)
        ring_send(0, left_order[p], False)
    send(head, hs.at[own], h_send.at[0], hx_recv.at[0], at(1, 0))
    send(head, hs.at[own], h_send.at[0], hx_recv.at[1], at(-1, 0))
    to_y(0, head)
    to_core(0, 0, head)
    mine = [
        pltpu.make_async_copy(feat, fs.at[z], local.at[0]),
        pltpu.make_async_copy(head, hs.at[own], local.at[1]),
        pltpu.make_async_copy(cap_in, cap, local.at[2]),
    ]
    for c in mine:
        c.start()

    def x_near():
        behind = slot(-way, 0)
        arrived(hs.at[behind], hx_recv.at[core])
        send(hs.at[behind], hs.at[behind], h_send.at[0], hx_recv.at[2], at(way, 0))
        arrived(hs.at[slot(way, 0)], hx_recv.at[1 - core])
        for j in (1, 2):
            to_y(j, hs.at[slot(x_off[j], 0)])
            to_core(j, 0, hs.at[slot(x_off[j], 0)])

    def x_far():
        arrived(hs.at[slot(2, 0)], hx_recv.at[2])
        to_y(3, hs.at[slot(2, 0)])
        to_core(3, 0, hs.at[slot(2, 0)])

    def y_pair(j):
        k = slot(x_off[j], -way)
        arrived(hs.at[k], hy_recv.at[j, core])
        send(hs.at[k], hs.at[k], h_send.at[0], hy_recv.at[j, 2], at(0, way))
        arrived(hs.at[slot(x_off[j], way)], hy_recv.at[j, 1 - core])
        to_core(j, 1, hs.at[slot(x_off[j], -1)])
        to_core(j, 2, hs.at[slot(x_off[j], 1)])

    def y_far(j):
        k = slot(x_off[j], 2)
        arrived(hs.at[k], hy_recv.at[j, 2])
        to_core(j, 3, hs.at[k])

    x_near()
    ring_step(1)
    y_pair(0)
    ring_step(2, range(PIECES // 2))
    x_far()
    ring_step(2, range(PIECES // 2, PIECES))
    y_far(0)
    y_pair(1)
    ring_step(3, range(PIECES // 2))
    y_pair(2)
    ring_step(3, range(PIECES // 2, PIECES))
    y_far(1)
    y_pair(3)
    ring_step(4, range(PIECES // 2))
    y_far(2)
    ring_step(4, range(PIECES // 2, PIECES))
    y_far(3)
    ring_step(5)

    def head_of(k):
        return hs[pl.ds(2 * k, 2)].reshape(slab, classes)

    def logits_of(slots, r0, count):
        left = jnp.concatenate([fs[k, pl.ds(r0, count), :] for k in slots], axis=1)
        right = jnp.concatenate([head_of(k) for k in slots], axis=0)
        return jnp.dot(left, right, preferred_element_type=F32)

    def around(*distances):
        return [lax.rem(z + d, groups) for e in distances for d in (groups - e, e)]

    ring_step(6)
    arrived(hs.at[pl.ds(0, 4 * SIDE)], hc_recv.at[0])
    for c in mine:
        c.wait()
    acc[...] = logits_of(around(1, 2), 0, rows)
    acc[...] += logits_of(around(3, 4), 0, rows)
    ring_step(7, range(PIECES // 2))
    acc[...] += logits_of(around(5, 6), 0, rows)
    ring_step(7, range(PIECES // 2, PIECES))
    acc[...] += logits_of(around(7), 0, rows)

    lanes = 128
    tiles = classes // lanes

    def lane_tiles(v):
        return [v[:, i * lanes:(i + 1) * lanes] for i in range(tiles)]

    def turned_sum(v):
        return jnp.sum(sum(lane_tiles(v)[1:], lane_tiles(v)[0]).T, axis=0, keepdims=True)

    opposite = lax.rem(z + far, groups)
    start_order = [q for pair in zip(right_order[: PIECES // 2], left_order[: PIECES // 2]) for q in pair]
    for q in start_order:
        ring_wait(far - 1, q, halfway(q, True))
        r0 = q * n
        block = pl.ds(r0, n)
        tanh = jnp.tanh((acc[block, :] + logits_of([z, opposite], r0, n)) / softcap)
        student = jnp.exp(softcap * tanh)
        transport = student * student
        stu[block, :] = student
        plan[block, :] = transport
        slope[block, :] = 1.0 - tanh * tanh
        zs0[:, r0:r0 + n] = turned_sum(transport)
        zs0[:, rows + r0:rows + r0 + n] = turned_sum(student)

    z_order = sorted(range(1, groups), key=lambda d: -min(d, groups - d))

    def z_exchange(mine, theirs, i):
        for d in z_order:
            copy(mine, theirs.at[d - 1], zsend.at[i], zrecv.at[i], along(d)).start()

    def z_total(mine, theirs, i):
        copy(theirs, theirs, zsend.at[i], zrecv.at[i], along(1)).wait_recv()
        return mine[...] + jnp.sum(theirs[...], axis=0)

    def c_exchange(mine, theirs, i):
        for n, (dx, dy, dc) in enumerate(OTHERS):
            copy(mine, theirs.at[n], csend.at[i], crecv.at[i], at(dx, dy, dc)).start()

    def c_total(mine, theirs, i):
        copy(theirs, theirs, csend.at[i], crecv.at[i], along(1)).wait_recv()
        return mine[...] + jnp.sum(theirs[...], axis=0)

    def upright(row, r0):
        return jnp.broadcast_to(row[:, r0:r0 + lanes], (lanes, lanes)).T

    z_exchange(zs0, zr0, 0)

    def turn(k, carry):
        t = fs[k].T
        for c in range(2):
            fta[c, lax.rem(k, SIDE), k // SIDE] = t[(2 * c) * quarter:(2 * c + 1) * quarter]
            ftb[c, k // SIDE, lax.rem(k, SIDE)] = t[(2 * c + 1) * quarter:(2 * c + 2) * quarter]
        ht[k] = head_of(k).T
        return carry

    lax.fori_loop(0, groups, turn, 0)
    for r0 in range(0, rows, lanes):
        for c0 in range(0, classes, lanes):
            plan_t[c0:c0 + lanes, r0:r0 + lanes] = plan[r0:r0 + lanes, c0:c0 + lanes].T
    left(fs.at[pl.ds(0, groups - 1)], ag_send.at[0])
    left(hs.at[pl.ds(0, hs.shape[0] - 1)], h_send.at[0])

    def early_share(w, r0, count):
        block = pl.ds(r0, count)
        early[w, 0, block, :] = jnp.dot(split[w, block, :], ht[opposite], preferred_element_type=F32).astype(BF)

    def pair_share(w, d):
        both = jnp.concatenate([ht[lax.rem(z + d, groups)], ht[lax.rem(z - d + groups, groups)]], axis=1)
        return jnp.dot(split[w], both, preferred_element_type=F32)

    def early_near(w):
        out = pair_share(w, far - 1).astype(BF)
        early[w, 1] = out[:, :slab]
        early[w, 2] = out[:, slab:]

    def early_send(w, level, q, right):
        i = 0 if right else 1
        src = beyond.at[w, i] if level == 2 else early.at[w, 0 if level == 0 else 1 + i]
        send(part_of(src, q), part_of(early_in.at[w, i, level], q), e_send.at[w],
             ring_recv.at[i, far - 2 + 2 * w + level % 2, q], along(1 if right else -1))

    def early_wait(w, level, q, right):
        i = 0 if right else 1
        arrived(part_of(early_in.at[w, i, level], q), ring_recv.at[i, far - 2 + 2 * w + level % 2, q])

    def early_fresh(w):
        for p in range(PIECES // 2):
            early_send(w, 1, left_order[p], True)
            early_send(w, 1, right_order[p], False)

    def early_pass(w):
        for p in range(PIECES // 2):
            for q, right in ((right_order[p], True), (left_order[p], False)):
                i = 0 if right else 1
                early_wait(w, 0, q, right)
                block = pl.ds(q * n, n)
                added = early[w, 1 + i, block, :].astype(F32) + early_in[w, i, 0, block, :].astype(F32)
                early[w, 1 + i, block, :] = added.astype(BF)
                early_send(w, 1, q, right)

    def late_shares(w):
        for m, d in enumerate((far - 2, far - 3)):
            late[w, m] = pair_share(w, d)

    def side(right):
        return slice(0, slab) if right else slice(slab, 2 * slab)

    def early_further(w):
        for p in range(PIECES // 2):
            for q, right in ((left_order[p], True), (right_order[p], False)):
                i = 0 if right else 1
                early_wait(w, 1, q, right)
                block = pl.ds(q * n, n)
                beyond[w, i, block, :] = (late[w, 0, block, side(right)] + early_in[w, i, 1, block, :].astype(F32)).astype(BF)
                early_send(w, 2, q, right)

    def while_columns_travel(it):
        if it == 0:
            for q in start_order:
                block = pl.ds(q * n, n)
                sup = jnp.concatenate([upright(student_inverse, q * n)] * tiles, axis=1)
                split[0, block, :] = (stu[block, :] * sup * slope[block, :]).astype(BF)
                early_share(0, q * n, n)
                early_send(0, 0, q, halfway(q, True))
            early_near(0)
            early_fresh(0)
        elif it == 1:
            early_pass(0)
        elif it == 2:
            late_shares(0)
            early_further(0)

    def while_last_rows_travel(scale):
        for q in start_order:
            block = pl.ds(q * n, n)
            split[1, block, :] = (plan[block, :] * scale * slope[block, :]).astype(BF)
            early_share(1, q * n, n)
            early_send(1, 0, q, halfway(q, True))
        early_near(1)
        early_fresh(1)
        late_shares(1)
        early_pass(1)
        early_further(1)

    ceiling = cap[...].astype(F32).reshape(1, classes) * ratio
    scale = jnp.ones((1, classes), F32)
    both = z_total(zs0, zr0, 0)
    mass = both[:, :rows]
    student_inverse = 1.0 / both[:, rows:]
    for it in range(ITERS):
        inverse = 1.0 / mass
        for c0 in range(0, classes, lanes):
            cs[it, :, c0:c0 + lanes] = turned_sum(plan_t[pl.ds(c0, lanes), :] * inverse)
        c_exchange(cs.at[it], cr.at[it], it)
        while_columns_travel(it)
        total = c_total(cs.at[it], cr.at[it], it)
        scale = jnp.minimum(scale, ceiling / total)
        for r0 in range(0, rows, lanes):
            zs[it, :, r0:r0 + lanes] = turned_sum(plan[pl.ds(r0, lanes), :] * scale)
        z_exchange(zs.at[it], zr.at[it], it + 1)
        if it == ITERS - 1:
            while_last_rows_travel(scale)
        mass = z_total(zs.at[it], zr.at[it], it + 1)

    def rs_send_to(d, q, right):
        i = 0 if right else 1
        src = part.at[d if right or d == far else groups - d]
        dst = from_l if right else from_r
        send(part_of(src, q), part_of(dst.at[d - 1], q), rs_send.at[0], ring_recv.at[i, d - 1, q],
             along(1 if right else -1))

    def rs_add(d, q, right):
        i = 0 if right else 1
        got = (from_l if right else from_r).at[d]
        mine = part.at[d if right else groups - d]
        arrived(part_of(got, q), ring_recv.at[i, d, q])
        block = pl.ds(q * n, n)
        mine[block, :] = (mine[block, :].astype(F32) + got[block, :].astype(F32)).astype(BF)
        rs_send_to(d, q, right)

    rs_events = [(far - 3, right_order[p], left_order[p]) for p in range(PIECES // 2)]
    rs_events += [(d, left_order[p], right_order[p]) for d in range(far - 4, 0, -1) for p in range(PIECES)]

    def share_pair(d):
        both = jnp.concatenate([ht[lax.rem(z + d, groups)], ht[lax.rem(z - d + groups, groups)]], axis=1)
        out = jnp.dot(grad[...], both, preferred_element_type=F32).astype(BF)
        part[d] = out[:, :slab]
        part[groups - d] = out[:, slab:]

    def share_own():
        part[0] = jnp.dot(grad[...], ht[z], preferred_element_type=F32).astype(BF)

    inverse = 1.0 / mass
    ups = [upright(inverse, q * n) for q in range(PIECES)]

    def merge(q, right, level):
        i = 0 if right else 1
        for w in range(2):
            early_wait(w, level, q, right)
        block = pl.ds(q * n, n)
        student_part, plan_part = (
            late[w, level - 1, block, side(right)] + early_in[w, i, level, block, :].astype(F32) for w in range(2)
        )
        d = far - 1 - level
        part[d if right else groups - d, block, :] = (student_part - ups[q] * plan_part).astype(BF)
        rs_send_to(d, q, right)

    for q in range(PIECES):
        block = pl.ds(q * n, n)
        up = jnp.concatenate([ups[q]] * tiles, axis=1)
        targets = (plan[block, :] * up * scale).astype(BF)
        tgt[block, :] = targets
        sup = jnp.concatenate([upright(student_inverse, q * n)] * tiles, axis=1)
        grad[block, :] = ((stu[block, :] * sup - targets.astype(F32)) * slope[block, :]).astype(BF)

    def next_shares():
        for p in range(PIECES // 2):
            for q, right, k in ((right_order[p], True, far - 3), (left_order[p], False, groups - far + 3)):
                block = pl.ds(q * n, n)
                part[k, block, :] = (late[0, 1, block, side(right)] - ups[q] * late[1, 1, block, side(right)]).astype(BF)

    def summed(*refs):
        out = refs[0].astype(F32)
        for r in refs[1:]:
            out = out + r.astype(F32)
        return out.astype(BF)

    fwd = 1 + 2 * core
    bwd = 3 - 2 * core

    def first_to(half, d):
        return at(d, 0) if half else at(0, d)

    def second_to(half, d):
        return at(0, d) if half else at(d, 0)

    def first_pos(half, d):
        return lax.rem((x if half else y) + d + SIDE, SIDE)

    def second_pos(half, d):
        return lax.rem((y if half else x) + d + SIDE, SIDE)

    def head_share(out, half, c, pair):
        turned = ftb if half else fta
        lhs = jnp.concatenate([turned[c, first_pos(half, i)].reshape(SIDE * quarter, rows) for i in pair], axis=0)
        share = jnp.dot(lhs, grad[...], preferred_element_type=F32).astype(BF)
        for n_, i in enumerate(pair):
            out[half, i] = share[n_ * SIDE * quarter:(n_ + 1) * SIDE * quarter].reshape(SIDE, quarter, classes)

    def give(half, pair):
        head_share(qo, half, 1 - core, pair)
        for i in pair:
            send(qo.at[half, i], core_in.at[half, i], qc_send.at[0], qc_recv.at[half, i], at(0, 0, 1))

    def keep(half):
        head_share(qa, half, core, (2, 1))
        head_share(qa, half, core, (3, 0))

    def chip_sum(half):
        for i in (2, 1, 3, 0):
            arrived(core_in.at[half, i], qc_recv.at[half, i])
            qa[half, i] = summed(qa[half, i], core_in[half, i])
            if i == 2:
                send(qa.at[half, 2], first_in.at[half, 0], q1_send.at[0], q1_recv.at[half, 0], first_to(half, way))
            if i == 3:
                send(qa.at[half, bwd], first_in.at[half, 1], q1_send.at[0], q1_recv.at[half, 1],
                     first_to(half, -way))

    def first_mid(half):
        arrived(first_in.at[half, 0], q1_recv.at[half, 0])
        qa[half, fwd] = summed(qa[half, fwd], first_in[half, 0])
        send(qa.at[half, fwd], first_in.at[half, 2], q1_send.at[0], q1_recv.at[half, 2], first_to(half, way))

    def first_end(half):
        arrived(first_in.at[half, 1], q1_recv.at[half, 1])
        arrived(first_in.at[half, 2], q1_recv.at[half, 2])
        qb[half] = summed(qa[half, 0], first_in[half, 1], first_in[half, 2])
        send(qb.at[half, second_pos(half, 2)], second_in.at[half, 0], q2_send.at[0], q2_recv.at[half, 0],
             second_to(half, way))
        send(qb.at[half, second_pos(half, -way)], second_in.at[half, 1], q2_send.at[0], q2_recv.at[half, 1],
             second_to(half, -way))

    def second_mid(half):
        arrived(second_in.at[half, 0], q2_recv.at[half, 0])
        k = second_pos(half, way)
        qb[half, k] = summed(qb[half, k], second_in[half, 0])
        send(qb.at[half, k], second_in.at[half, 2], q2_send.at[0], q2_recv.at[half, 2], second_to(half, way))

    def second_end(half):
        arrived(second_in.at[half, 1], q2_recv.at[half, 1])
        arrived(second_in.at[half, 2], q2_recv.at[half, 2])
        total = summed(qb[half, second_pos(half, 0)], second_in[half, 1], second_in[half, 2])
        ghead[half * quarter:(half + 1) * quarter, :] = total

    give(0, (2, 1))
    give(0, (3, 0))
    for p in range(PIECES // 2):
        merge(right_order[p], True, 1)
        merge(left_order[p], False, 1)
    give(1, (2, 1))
    give(1, (3, 0))
    keep(0)
    for p in range(PIECES // 2):
        merge(left_order[p], True, 2)
        merge(right_order[p], False, 2)
    next_shares()
    keep(1)
    chip_sum(0)
    between = {
        0: [(share_pair, 4)], 1: [(chip_sum, 1)], 3: [(share_pair, 3)], 4: [(share_pair, 2)], 5: [(share_pair, 1)],
        6: [(share_own,)], 7: [(first_mid, 0)], 8: [(first_mid, 1)], 12: [(first_end, 0)], 13: [(first_end, 1)],
        16: [(second_mid, 0)], 17: [(second_mid, 1)],
    }
    for e, (d, to_right, to_left) in enumerate(rs_events):
        if e == 12:
            for w in range(2):
                left(part.at[pl.ds(0, 4)], e_send.at[w])
            left(qo, qc_send.at[0])
        rs_add(d, to_right, True)
        rs_add(d, to_left, False)
        for task, *what in between.get(e, ()):
            task(*what)

    for p in range(PIECES):
        arrived(part_of(from_l.at[0], left_order[p]), ring_recv.at[0, 0, left_order[p]])
        arrived(part_of(from_r.at[0], right_order[p]), ring_recv.at[1, 0, right_order[p]])
    second_end(0)
    second_end(1)
    gfeat[...] = summed(part[0], from_l[0], from_r[0])

    copy(zr0, zr0, zsend.at[0], zrecv.at[0], along(1)).wait_send()
    for it in range(ITERS):
        copy(zr.at[it], zr.at[it], zsend.at[it + 1], zrecv.at[it + 1], along(1)).wait_send()
        copy(cr.at[it], cr.at[it], csend.at[it], crecv.at[it], along(1)).wait_send()
    left(part.at[pl.ds(0, far + 3)], rs_send.at[0])
    left(first_in, q1_send.at[0])
    left(second_in, q2_send.at[0])


def store_kernel(*refs):
    count = len(refs) // 2
    copies = []
    for i in range(count):
        parts = 4 if i == 0 else 1
        rows = refs[i].shape[0] // parts
        for p in range(parts):
            block = pl.ds(p * rows, rows)
            copies.append(pltpu.make_async_copy(refs[i].at[block], refs[count + i].at[block], refs[-1].at[len(copies)]))
    for c in copies:
        c.start()
    for c in copies:
        c.wait()


def store(results):
    return pl.pallas_call(
        store_kernel,
        out_shape=tuple(jax.ShapeDtypeStruct(r.shape, r.dtype) for r in results),
        in_specs=[pl.BlockSpec(memory_space=pltpu.VMEM)] * len(results),
        out_specs=(pl.BlockSpec(memory_space=pltpu.HBM),) * len(results),
        scratch_shapes=[pltpu.SemaphoreType.DMA((len(results) + 3,))],
        compiler_params=pltpu.CompilerParams(vmem_limit_bytes=4 << 20),
    )(*results)


def solution(mesh):
    groups = mesh.shape["cls"]
    samples = mesh.shape["sample"]

    def per_device(features, head, class_cap):
        rows, slab = features.shape
        depth, classes = head.shape
        width = slab * groups
        chips = samples // 2
        far = groups // 2
        ratio = rows * samples / (classes * groups)
        V = pltpu.VMEM
        dma = pltpu.SemaphoreType.DMA
        scratch = [
            V((groups, rows, slab), BF), V((samples, depth, classes), BF),
            V((2, SIDE, SIDE, depth // 2, rows), BF), V((2, SIDE, SIDE, depth // 2, rows), BF), V((groups, classes, slab), BF),
            V((rows, classes), F32), V((rows, classes), F32), V((rows, classes), F32), V((classes, rows), F32),
            V((rows, classes), F32),
            V((rows, classes), BF),
            V((groups, rows, slab), BF), V((far, rows, slab), BF), V((far, rows, slab), BF),
            V((2, rows, classes), BF), V((2, 3, rows, slab), BF), V((2, 2, 3, rows, slab), BF), V((2, 2, rows, 2 * slab), F32),
            V((2, 2, rows, slab), BF),
            V((2, SIDE, SIDE, depth // 2, classes), BF), V((2, SIDE, SIDE, depth // 2, classes), BF),
            V((2, SIDE, SIDE, depth // 2, classes), BF), V((2, 3, SIDE, depth // 2, classes), BF),
            V((2, SIDE, depth // 2, classes), BF), V((2, 3, depth // 2, classes), BF),
            V((1, 2 * rows), F32), V((ITERS, 1, rows), F32),
            V((groups - 1, 1, 2 * rows), F32), V((ITERS, groups - 1, 1, rows), F32),
            V((ITERS, 1, classes), F32), V((ITERS, samples - 1, 1, classes), F32),
            dma((1,)), dma((2, far + 2, PIECES)), dma((1,)), dma((3,)), dma((4, 3)), dma((1,)),
            dma((ITERS + 1,)), dma((ITERS + 1,)), dma((ITERS,)), dma((ITERS,)),
            V((classes,), BF), dma((3,)), dma((2,)),
            dma((1,)), dma((1,)), dma((2, 4)), dma((1,)), dma((2, 3)), dma((1,)), dma((2, 3)),
        ]
        vmem = pl.BlockSpec(memory_space=pltpu.VMEM)
        hbm = pl.BlockSpec(memory_space=pltpu.HBM)
        results = pl.pallas_call(
            functools.partial(kernel, rows, width, classes, groups, ratio),
            out_shape=(
                jax.ShapeDtypeStruct((rows, classes), BF),
                jax.ShapeDtypeStruct((rows, slab), BF),
                jax.ShapeDtypeStruct((depth, classes), BF),
            ),
            in_specs=[hbm] * 3,
            out_specs=(vmem,) * 3,
            scratch_shapes=scratch,
            compiler_params=pltpu.CompilerParams(
                collective_id=0, has_side_effects=True, vmem_limit_bytes=48 << 20
            ),
        )(*(pltpu.with_memory_space_constraint(a, pltpu.HBM) for a in (features, head, class_cap)))
        return store(results)

    return jax.shard_map(
        per_device,
        mesh=mesh,
        in_specs=(P("sample", "cls"), P("sample", "cls"), P("cls")),
        out_specs=(P("sample", "cls"), P("sample", "cls"), P("sample", "cls")),
        check_vma=False,
    )
```
